32 devices in a mesh: scen: 4 (over y, core), row: 8 (over z, x).
Axes of the slice: x: 2, y: 2, z: 4, core: 2. Of those that a mesh axis runs over, the one named last changes fastest.
Arguments:
- borders: bfloat16 [4, 1024, 12288], P('scen', None, 'row'), may hold values from -1.078125 to 1.078125
- kkt_inverse: bfloat16 [4, 1024, 1024], P('scen', 'row'), may hold values from -0.35 to 2.35, as said below
- first_section: float32 [12288, 256], P('row'), may hold values from -6 to 6
- barrier: float32 [12288], P('row'), may hold values from 64 to 512
- panel_vars: int32 [256], replicated, may hold values from 0 to 12287, as said below
- probability: float32 [4], replicated, may hold values from 0.5 to 2
- assignment: int32 [4], P('scen'), may hold values from 0 to 3, each once
Outputs:
- factor: float32 [12288, 256], P('row')
The draws below stay inside these ranges and needn't reach their ends.
Inputs may be any that keep to these rules, and one draw needn't show every extreme that they name: `panel_vars`: distinct values. `kkt_inverse`: each scenario's matrix is symmetric positive definite. `assignment`: each scenario once.
All inputs are finite; a program needn't handle non-finite values.
Results may differ from the reference program's by a relative error of at most 0.00031.
Values may be sent and summed in bfloat16 or wider, within the bound.
A program may use at most 64 MiB of HBM per device.

```python
import math
import jax
import jax.numpy as jnp
from jax import lax

N0 = 12288
NS = 1024
PANEL = 128
PANELS = 2
WIN = 256
SCENARIOS = 4


def draw_panel_vars(key, part):
    chosen = jax.random.permutation(jax.random.fold_in(key, 11), N0)
    return chosen[:WIN].astype(jnp.int32)


def draw_kkt_inverse(key, part):
    noise_key, diag_key = jax.random.split(jax.random.fold_in(key, 23))
    noise = jnp.clip(jax.random.normal(noise_key, (SCENARIOS, NS, NS), jnp.float32), -3.0, 3.0)
    symmetric = (noise + jnp.swapaxes(noise, 1, 2)) * (0.4 / math.sqrt(2.0 * NS))
    diagonal = jnp.exp(jax.random.uniform(diag_key, (SCENARIOS, NS), jnp.float32, 0.0, math.log(2.0)))
    result = symmetric + diagonal[:, :, None] * jnp.eye(NS, dtype=jnp.float32)[None, :, :]
    return result.astype(jnp.bfloat16)


def levels(rng, extent, cuts, smallest, high):
    def one(position, parts):
        draws = jax.random.uniform(jax.random.fold_in(jax.random.fold_in(rng, 6), position), (parts,), jnp.float32, smallest / len(cuts), high / len(cuts))
        return jnp.repeat(jnp.exp(draws), extent[position] // parts).reshape((-1,) + (1,) * (len(extent) - position - 1))

    level = one(*cuts[0])
    for cut in cuts[1:]:
        level = level * one(*cut)
    return level


def normal_values(rng, extent, deviation, reach, pieces=(), kind=jnp.bfloat16):
    loudness = levels(rng, extent, pieces, -0.22, 0.18) if pieces else 1.0
    entries = jax.random.normal(rng, extent, jnp.float32) * deviation * loudness
    return jnp.minimum(jnp.maximum(entries, -reach), reach).astype(kind)


def setup_inputs(seed: int = 0) -> dict:
    streams_of = jax.random.split(jax.random.key(seed), 8)
    return {
        "borders": normal_values(streams_of[0], (SCENARIOS, NS, N0), 0.18, 1.078125, ((0, 4), (2, 8))),
        "kkt_inverse": draw_kkt_inverse(jax.random.fold_in(streams_of[7], 71), 0),
        "first_section": normal_values(streams_of[2], (N0, WIN), 1.0, 6.0, ((0, 8),), jnp.float32),
        "barrier": jnp.clip(jnp.exp(math.log(512.0) - 2.0794415 * jax.random.uniform(streams_of[3], (N0,), jnp.float32) ** levels(streams_of[3], (N0,), ((0, 8),), -0.2, 0.2)), 64.0, 512.0),
        "panel_vars": draw_panel_vars(jax.random.fold_in(streams_of[7], 71), 0),
        "probability": jnp.clip(jnp.exp(jax.random.uniform(streams_of[5], (SCENARIOS,), jnp.float32, math.log(0.5), math.log(2.0))), 0.5, 2.0),
        "assignment": jax.random.permutation(streams_of[6], SCENARIOS).astype(jnp.int32),
    }


def factorize(diag_block, row_block):
    symmetric = 0.5 * (diag_block + diag_block.T)
    block_parts = []
    row_parts = []
    for panel_index in range(PANELS):
        low_col = panel_index * PANEL
        high_col = low_col + PANEL
        block_cols = symmetric[:, low_col:high_col]
        row_cols = row_block[:, low_col:high_col]
        if panel_index > 0:
            earlier_block = jnp.concatenate(block_parts, axis=1)
            earlier_rows = jnp.concatenate(row_parts, axis=1)
            across = earlier_block[low_col:high_col, :]
            block_cols = block_cols - jnp.dot(earlier_block, across.T, precision=lax.Precision.HIGHEST)
            row_cols = row_cols - jnp.dot(earlier_rows, across.T, precision=lax.Precision.HIGHEST)
        panel_chol = jnp.linalg.cholesky(block_cols[low_col:high_col, :])
        block_parts.append(lax.linalg.triangular_solve(panel_chol, block_cols, left_side=False, lower=True, transpose_a=True))
        row_parts.append(lax.linalg.triangular_solve(panel_chol, row_cols, left_side=False, lower=True, transpose_a=True))
    return jnp.concatenate(row_parts, axis=1)

def reference(borders, kkt_inverse, first_section, barrier, panel_vars, probability, assignment):
    scen_count = borders.shape[0]
    picked = jnp.take(borders, panel_vars, axis=2)
    weights = jnp.take(probability, assignment)

    def accumulate(scen_index, total):
        inverse = lax.dynamic_index_in_dim(kkt_inverse, scen_index, 0, keepdims=False)
        columns = lax.dynamic_index_in_dim(picked, scen_index, 0, keepdims=False)
        border = lax.dynamic_index_in_dim(borders, scen_index, 0, keepdims=False)
        solved = jnp.dot(inverse.astype(jnp.float32), columns.astype(jnp.float32), preferred_element_type=jnp.float32).astype(jnp.bfloat16)
        term = lax.dot_general(border.astype(jnp.float32), solved.astype(jnp.float32), (((0,), (0,)), ((), ())), preferred_element_type=jnp.float32)
        return total + weights[scen_index] * term
    total = lax.fori_loop(0, scen_count, accumulate, jnp.zeros((N0, WIN), jnp.float32))
    hits = jnp.arange(N0, dtype=jnp.int32)[:, None] == panel_vars[None, :]
    schur = total + first_section + jnp.where(hits, barrier[:, None], jnp.zeros((), jnp.float32))
    diag_block = jnp.take(schur, panel_vars, axis=0)
    return factorize(diag_block, schur)
```

```python
import functools

import jax
import jax.numpy as jnp
from jax import lax
from jax.experimental import pallas as pl
from jax.experimental.pallas import tpu as pltpu
from jax.sharding import PartitionSpec as P

PANEL = 128
MESH = pl.DeviceIdType.MESH
HIGH = lax.Precision.HIGHEST
F32 = jnp.float32
BF16 = jnp.bfloat16
PARTS = 3
SUB = 8
BLOCK = 32


def small_factor(tile, first):
    shape = tile.shape
    spread = [
        jnp.broadcast_to(tile[:, first + k:first + k + 1], shape) for k in range(SUB)
    ]
    cell = {
        (i, k): jnp.broadcast_to(spread[k][i:i + 1, :], shape)
        for k in range(SUB) for i in range(k, SUB)
    }
    scale, lower = [], {}
    for j in range(SUB):
        scale.append(lax.rsqrt(cell[j, j]))
        for i in range(j + 1, SUB):
            lower[i, j] = cell[i, j] * scale[j]
        for k in range(j + 1, SUB):
            for i in range(k, SUB):
                cell[i, k] = cell[i, k] - lower[i, j] * lower[k, j]
    inverse = {}
    for j in range(SUB):
        inverse[j, j] = scale[j]
        for i in range(j + 1, SUB):
            total = lower[i, j] * inverse[j, j]
            for m in range(j + 1, i):
                total = total + lower[i, m] * inverse[m, j]
            inverse[i, j] = -(scale[i] * total)
    return inverse


def panel_inverse(block, size, hook=None):
    panel = block.shape[0]
    shape = (SUB, panel)
    sub = lax.broadcasted_iota(jnp.int32, shape, 0)
    lane = lax.broadcasted_iota(jnp.int32, shape, 1)
    tiles = panel // SUB
    left = [block[low:low + SUB, :] for low in range(0, panel, SUB)]
    right = [jnp.where(lane == sub + low, 1.0, 0.0) for low in range(0, panel, SUB)]
    per = size // SUB
    for base in range(0, tiles, per):
        for own in range(base, base + per):
            first = own * SUB
            inverse = small_factor(left[own], first)
            new_left = new_right = None
            for k in range(SUB):
                coeff = inverse[SUB - 1, k]
                for i in range(SUB - 2, k - 1, -1):
                    coeff = jnp.where(sub <= i, inverse[i, k], coeff)
                if k:
                    coeff = jnp.where(sub < k, 0.0, coeff)
                add_left = coeff * left[own][k:k + 1, :]
                add_right = coeff * right[own][k:k + 1, :]
                new_left = add_left if k == 0 else new_left + add_left
                new_right = add_right if k == 0 else new_right + add_right
            for tile in range(own + 1, base + per):
                spread = [
                    jnp.broadcast_to(left[tile][:, first + m:first + m + 1], shape)
                    for m in range(SUB)
                ]
                for k in range(SUB):
                    factor = spread[0] * inverse[k, 0]
                    for m in range(1, k + 1):
                        factor = factor + spread[m] * inverse[k, m]
                    left[tile] = left[tile] - factor * new_left[k:k + 1, :]
                    right[tile] = right[tile] - factor * new_right[k:k + 1, :]
            left[own], right[own] = new_left, new_right
        if base + per < tiles:
            upper = jnp.concatenate(left[base:base + per], axis=0)
            both = jnp.concatenate(
                [upper, jnp.concatenate(right[base:base + per], axis=0)], axis=1
            )
            change = lax.dot_general(
                upper, both, (((0,), (0,)), ((), ())),
                precision=HIGH, preferred_element_type=F32,
            )
            for tile in range(base + per, tiles):
                low = tile * SUB
                left[tile] = left[tile] - change[low:low + SUB, :panel]
                right[tile] = right[tile] - change[low:low + SUB, panel:]
        if hook is not None:
            hook(base // per)
    return jnp.concatenate(right, axis=0)


def flip(index, bit):
    return index + bit * (1 - 2 * ((index // bit) % 2))


def toggle(index, mask):
    bit = 1
    while bit <= mask:
        if mask & bit:
            index = flip(index, bit)
        bit *= 2
    return index


def bits_down(count):
    bits = []
    bit = count // 2
    while bit >= 1:
        bits.append(bit)
        bit //= 2
    return bits


def low_bit(mask):
    return mask & -mask


def split3(value):
    high = value.astype(BF16)
    rest = value - high.astype(F32)
    middle = rest.astype(BF16)
    low = (rest - middle.astype(F32)).astype(BF16)
    return high, middle, low


def matmul_t(lhs, rhs):
    return lax.dot_general(
        lhs, rhs, (((1,), (1,)), ((), ())),
        precision=HIGH, preferred_element_type=F32,
    )


def schur_kernel(
    n_scen, n_row,
    pv_row, pv_s, prob, asg, bar_row, b_hbm, k_hbm, base_hbm,
    out_ref,
    b_ref, k_ref, base, load_sem, rest_sem, onehot,
    picked, xin, zsum, zin, columns, solved,
    fpick, fxin, fsum, fzin, fall,
    bt, ct, tf, t_sum, t_in,
    out_half, in_half, mine, y_in, hbuf,
    rsx_send, rsx_recv, rsz_send, rsz_recv,
    cz_send, cz_recv, cx_send, cx_recv,
    sz_send, sz_recv, sx_send, sx_recv,
    t_send, t_recv, c_send, c_recv, y_send, y_recv, g_send, g_recv,
):
    scen = lax.axis_index("scen")
    row = lax.axis_index("row")
    panels = columns.shape[0]
    depth = columns.shape[2]
    full = n_row * depth
    rows, window = base.shape
    nz = n_row // 2
    z, x = row // 2, row % 2
    other = flip(row, 1)
    barrier = pltpu.get_barrier_semaphore()
    scen_bits = bits_down(n_scen)[::-1]
    y_bits = scen_bits[1:]
    near = [toggle(z, step) for step in range(1, nz)]
    far = near[::-1]
    frow = fpick.shape[1]
    frows = n_row * frow
    groups = window // frows
    fstart = (scen % groups) * frows
    first = row * rows
    sent, given = [], {}

    pl.semaphore_signal(barrier, inc=1, device_id={"row": other}, device_id_type=MESH)
    for peer in far:
        pl.semaphore_signal(
            barrier, inc=1, device_id={"row": 2 * peer + x}, device_id_type=MESH
        )
    for bit in scen_bits:
        pl.semaphore_signal(
            barrier, inc=1, device_id={"scen": flip(scen, bit)}, device_id_type=MESH
        )

    def load(block):
        start = pl.multiple_of(block * depth, depth)
        return pltpu.make_async_copy(
            b_hbm.at[pl.ds(start, depth), :],
            b_ref.at[pl.ds(start, depth), :],
            load_sem.at[block],
        )

    base_load = pltpu.make_async_copy(base_hbm, base, rest_sem.at[0])
    k_load = pltpu.make_async_copy(k_hbm, k_ref, rest_sem.at[1])
    for peer in far + [z]:
        load(2 * peer + 1 - x).start()
    for peer in far + [z]:
        load(2 * peer + x).start()
    base_load.start()
    k_load.start()

    onehot[...] = jnp.where(
        lax.broadcasted_iota(jnp.int32, (rows, window), 0) == pv_row[...] - first,
        1.0, 0.0,
    ).astype(BF16)
    bar = split3(bar_row[...].reshape(1, rows))
    level = lax.broadcasted_iota(jnp.int32, (2 * SUB, rows), 0)
    bars = jnp.where(
        level == 0, bar[0].astype(F32),
        jnp.where(level == 1, bar[1].astype(F32),
                  jnp.where(level == 2, bar[2].astype(F32), 0.0)),
    ).astype(BF16)

    pl.semaphore_wait(barrier, nz + len(scen_bits))

    def remote(src, dst, send, recv, where):
        return pltpu.make_async_remote_copy(
            src_ref=src, dst_ref=dst, send_sem=send, recv_sem=recv,
            device_id=where, device_id_type=MESH,
        )

    def go(copy):
        copy.start()
        sent.append(copy)

    pick_of = [picked.at[p] for p in range(panels)] + [fpick]
    xin_of = [xin.at[p] for p in range(panels)] + [fxin]
    zsum_of = [zsum.at[p] for p in range(panels)] + [fsum]
    zin_of = [zin.at[p] for p in range(panels)] + [fzin]
    col_of = [columns.at[p] for p in range(panels)] + [fall]
    sol_of = [solved.at[p] for p in range(panels)]

    def rsx(p, peer):
        return remote(
            pick_of[p].at[2 * peer + 1 - x], xin_of[p].at[peer],
            rsx_send.at[p, peer], rsx_recv.at[p, peer], {"row": other},
        )

    def rsz_go(p, peer):
        go(remote(
            zsum_of[p].at[peer], zin_of[p].at[z],
            rsz_send.at[p, peer], rsz_recv.at[p, z], {"row": 2 * peer + x},
        ))

    def rsz_wait(p, peer):
        remote(
            zsum_of[p].at[peer], zin_of[p].at[peer],
            rsz_send.at[p, peer], rsz_recv.at[p, peer], {"row": 2 * peer + x},
        ).wait_recv()

    def rs_turn(p):
        for peer in far + [z]:
            rsx(p, peer).wait_recv()
            zsum_of[p][peer] = pick_of[p][2 * peer + x] + xin_of[p][peer]
            if peer is not z:
                rsz_go(p, peer)

    def rs_end(p):
        total = zsum_of[p][z].astype(F32)
        for peer in near:
            rsz_wait(p, peer)
            total = total + zin_of[p][peer].astype(F32)
        col_of[p][row] = total.astype(col_of[p].dtype)

    cols = (col_of, cz_send, cz_recv, cx_send, cx_recv)
    sols = (sol_of, sz_send, sz_recv, sx_send, sx_recv)

    def ag_x(kind, p, peer):
        held, _, _, xs, xr = kind
        return remote(
            held[p].at[2 * peer + x], held[p].at[2 * peer + x],
            xs.at[p, peer], xr.at[p, peer], {"row": other},
        )

    def ag_start(kind, p):
        held, zs, zr, _, _ = kind
        for peer in far:
            go(remote(
                held[p].at[row], held[p].at[row],
                zs.at[p, peer], zr.at[p, z], {"row": 2 * peer + x},
            ))
        go(ag_x(kind, p, z))

    def ag_pass(kind, p, peer):
        held, zs, zr, _, _ = kind
        remote(
            held[p].at[2 * peer + x], held[p].at[2 * peer + x],
            zs.at[p, peer], zr.at[p, peer], {"row": 2 * peer + x},
        ).wait_recv()
        go(ag_x(kind, p, peer))

    def ag_end(kind, p):
        held, _, _, xs, xr = kind
        for peer in [z] + near:
            remote(
                held[p].at[2 * peer + 1 - x], held[p].at[2 * peer + 1 - x],
                xs.at[p, peer], xr.at[p, peer], {"row": other},
            ).wait_recv()

    def pick(dst):
        load(dst).wait()
        start = pl.multiple_of(dst * depth, depth)
        block = jnp.dot(
            b_ref[pl.ds(start, depth), :], onehot[...], preferred_element_type=F32
        ).astype(BF16)
        for p in range(panels):
            picked[p, dst] = block[:, p * PANEL:(p + 1) * PANEL]

    for peer in far + [z]:
        pick(2 * peer + 1 - x)
        go(rsx(0, peer))
    for p in range(1, panels):
        for peer in far + [z]:
            go(rsx(p, peer))
    for peer in far + [z]:
        pick(2 * peer + x)

    for p in range(panels):
        rs_turn(p)

    bsel = jnp.sum(
        jnp.dot(bars, onehot[...], preferred_element_type=F32), axis=0, keepdims=True
    )
    base_load.wait()
    slot_row = lax.broadcasted_iota(jnp.int32, (frow, window), 0) + fstart
    slot_col = lax.broadcasted_iota(jnp.int32, (frow, window), 1)

    def frag(block, carry):
        lines = []
        for i in range(frow):
            at = pv_s[fstart + block * frow + i] - first
            inside = jnp.logical_and(at >= 0, at < rows)
            line = base[pl.ds(jnp.clip(at, 0, rows - 1), 1), :]
            lines.append(jnp.where(inside, line, 0.0))
        fpick[block] = jnp.concatenate(lines, axis=0) + jnp.where(
            slot_row + block * frow == slot_col, bsel, 0.0
        )
        return carry

    lax.fori_loop(0, n_row, frag, 0)
    for peer in far + [z]:
        go(rsx(panels, peer))

    def turn(tile, carry):
        start = pl.multiple_of(tile * PANEL, PANEL)
        bt[pl.ds(start, PANEL), :] = b_ref[:, pl.ds(start, PANEL)].T
        return carry

    lax.fori_loop(0, rows // PANEL, turn, 0)

    rs_end(0)
    ag_start(cols, 0)
    base[...] += onehot[...].astype(F32) * bsel
    rs_turn(panels)
    ag_pass(cols, 0, near[0])
    rs_end(1)
    ag_start(cols, 1)
    for peer in near[1:]:
        ag_pass(cols, 0, peer)
    rs_end(panels)
    ag_start(cols, panels)
    k_load.wait()
    ag_pass(cols, 1, near[0])

    def solve(p):
        solved[p, row] = jnp.dot(
            k_ref[...], columns[p].reshape(full, PANEL), preferred_element_type=F32
        ).astype(BF16)

    def side(p):
        ct[p] = columns[p].reshape(full, PANEL).T

    ag_end(cols, 0)
    solve(0)
    ag_start(sols, 0)
    for peer in near[1:]:
        ag_pass(cols, 1, peer)
    side(0)
    ag_pass(sols, 0, near[0])
    for peer in near:
        ag_pass(cols, panels, peer)
    ag_end(cols, 1)
    solve(1)
    ag_start(sols, 1)
    for peer in near[1:]:
        ag_pass(sols, 0, peer)
    side(1)
    ag_end(cols, panels)
    tf[...] = jnp.zeros_like(tf)
    keep = jnp.where(scen < groups, 1.0, 0.0)
    tf[pl.ds(pl.multiple_of(fstart, SUB), frows), :] = fall[...].reshape(frows, window) * keep
    match = lax.broadcasted_iota(jnp.int32, prob.shape, 1) == asg[...]
    weight = jnp.sum(jnp.where(match, prob[...], 0.0), axis=1, keepdims=True)
    for peer in near[:-1]:
        ag_pass(sols, 1, peer)

    def t_block(p, q):
        return weight * jnp.dot(
            ct[p], solved[q].reshape(full, PANEL), preferred_element_type=F32
        ) + tf[p * PANEL:(p + 1) * PANEL, q * PANEL:(q + 1) * PANEL]

    spans = [pl.ds(0, PANEL), pl.ds(PANEL, 2 * PANEL)]

    def t_copy(which, index):
        return remote(
            t_sum.at[index, spans[which]], t_in.at[index, spans[which]],
            t_send.at[which, index], t_recv.at[which, index],
            {"scen": flip(scen, scen_bits[index])},
        )

    def t_step(which, index):
        t_copy(which, index).wait_recv()
        t_sum[index + 1, spans[which]] = (
            t_sum[index, spans[which]] + t_in[index, spans[which]]
        )
        if index + 1 < len(scen_bits):
            go(t_copy(which, index + 1))

    core = scen % 2
    half = rows // 2
    chunk = half // PARTS
    parts = range(PARTS)

    def place(which, part):
        return pl.ds(pl.multiple_of(which * half + part * chunk, SUB), chunk)

    def term(which, p, part):
        return weight * jnp.dot(
            bt[place(which, part), :], solved[p].reshape(full, PANEL),
            preferred_element_type=F32,
        )

    def c_copy(p, part):
        return remote(
            out_half.at[p, part], in_half.at[p, part],
            c_send.at[p, part], c_recv.at[p, part], {"scen": flip(scen, 1)},
        )

    def y_copy(index, p, part):
        return remote(
            mine.at[index, p, part], y_in.at[index, p, part],
            y_send.at[index, p, part], y_recv.at[index, p, part],
            {"scen": flip(scen, y_bits[index])},
        )

    def g_copy(p, part, which):
        return remote(
            hbuf.at[p, place(which, part)], hbuf.at[p, place(which, part)],
            g_send.at[p, part], g_recv.at[p, part], {"scen": flip(scen, 1)},
        )

    def h_out(p):
        for part in parts:
            out_half[p, part] = term(1 - core, p, part)
            go(c_copy(p, part))

    def h_mine(p):
        for part in parts:
            mine[0, p, part] = term(core, p, part)

    def h_join(p, part):
        c_copy(p, part).wait_recv()
        mine[0, p, part] += in_half[p, part]
        go(y_copy(0, p, part))

    def y_step(p, part):
        for index in range(len(y_bits)):
            y_copy(index, p, part).wait_recv()
            total = mine[index, p, part] + y_in[index, p, part]
            if index + 1 < len(y_bits):
                mine[index + 1, p, part] = total
                go(y_copy(index + 1, p, part))
            else:
                hbuf[p, place(core, part)] = (
                    total + base[place(core, part), p * PANEL:(p + 1) * PANEL]
                )
                give = g_copy(p, part, core)
                give.start()
                given[p, part] = give

    ag_end(sols, 0)
    whole = t_block(0, 0)
    t_sum[0, spans[0]] = 0.5 * (whole + whole.T)
    go(t_copy(0, 0))
    for peer in near[-1:]:
        ag_pass(sols, 1, peer)
    h_out(0)
    t_step(0, 0)
    h_mine(0)
    h_join(0, 0)

    ag_end(sols, 1)
    t_sum[0, PANEL:2 * PANEL] = 0.5 * (t_block(1, 0) + t_block(0, 1).T)
    whole = t_block(1, 1)
    t_sum[0, 2 * PANEL:] = 0.5 * (whole + whole.T)
    go(t_copy(1, 0))
    h_out(1)
    t_step(1, 0)
    for part in parts[1:]:
        h_join(0, part)
    for index in range(1, len(scen_bits)):
        t_step(0, index)
    last = len(scen_bits)
    inverse_0 = panel_inverse(t_sum[last, spans[0]], BLOCK)
    for index in range(1, len(scen_bits)):
        t_step(1, index)
    h_mine(1)
    for part in parts:
        h_join(1, part)
    lower = matmul_t(t_sum[last, PANEL:2 * PANEL], inverse_0)
    block = t_sum[last, 2 * PANEL:] - matmul_t(lower, lower)

    def hook(stage):
        if stage < PARTS:
            y_step(0, stage)

    inverse_1 = panel_inverse(block, BLOCK, hook)

    def drop(p, which, part):
        if p == 0:
            left = matmul_t(hbuf[0, place(which, part)], inverse_0)
            out_ref[place(which, part), :PANEL] = left
            hbuf[0, place(which, part)] = matmul_t(left, lower)
        else:
            rest = hbuf[1, place(which, part)] - hbuf[0, place(which, part)]
            out_ref[place(which, part), PANEL:] = matmul_t(rest, inverse_1)

    for part in parts:
        g_copy(0, part, 1 - core).wait_recv()
        drop(0, 1 - core, part)
    for part in parts:
        given.pop((0, part)).wait_send()
        drop(0, core, part)
    for part in parts:
        y_step(1, part)
        drop(1, core, part)
    for part in parts:
        g_copy(1, part, 1 - core).wait_recv()
        drop(1, 1 - core, part)
    for one in sent + list(given.values()):
        one.wait_send()


def per_device(
    n_scen, n_row,
    borders, kkt_inverse, first_section, barrier, panel_vars, probability, assignment,
):
    rows, window = first_section.shape
    depth = kkt_inverse.shape[1]
    full = kkt_inverse.shape[2]
    panels = window // PANEL
    nz = n_row // 2
    groups = max(1, min(n_scen, window // (8 * n_row)))
    frow = window // groups // n_row
    stages = n_scen.bit_length() - 1
    chunk = rows // 2 // PARTS
    dma = pltpu.SemaphoreType.DMA
    vmem = pl.BlockSpec(memory_space=pltpu.VMEM)
    smem = pl.BlockSpec(memory_space=pltpu.SMEM)

    def buf(shape, dtype):
        return pltpu.VMEM(shape, dtype)

    return pl.pallas_call(
        functools.partial(schur_kernel, n_scen, n_row),
        out_shape=jax.ShapeDtypeStruct((rows, window), F32),
        in_specs=[vmem, smem] + [vmem] * 3 + [pl.BlockSpec(memory_space=pl.ANY)] * 3,
        out_specs=vmem,
        scratch_shapes=[
            buf((full, rows), BF16), buf((depth, full), BF16), buf((rows, window), F32),
            dma((n_row,)), dma((2,)), buf((rows, window), BF16),
            buf((panels, n_row, depth, PANEL), BF16),
            buf((panels, nz, depth, PANEL), BF16),
            buf((panels, nz, depth, PANEL), BF16),
            buf((panels, nz, depth, PANEL), BF16),
            buf((panels, n_row, depth, PANEL), BF16),
            buf((panels, n_row, depth, PANEL), BF16),
            buf((n_row, frow, window), F32),
            buf((nz, frow, window), F32),
            buf((nz, frow, window), F32),
            buf((nz, frow, window), F32),
            buf((n_row, frow, window), F32),
            buf((rows, full), BF16), buf((panels, PANEL, full), BF16),
            buf((window, window), F32),
            buf((stages + 1, 3 * PANEL, PANEL), F32),
            buf((stages, 3 * PANEL, PANEL), F32),
            buf((panels, PARTS, chunk, PANEL), F32),
            buf((panels, PARTS, chunk, PANEL), F32),
            buf((stages - 1, panels, PARTS, chunk, PANEL), F32),
            buf((stages - 1, panels, PARTS, chunk, PANEL), F32),
            buf((panels, rows, PANEL), F32),
            *[dma((panels + 1, nz))] * 8,
            *[dma((panels, nz))] * 4,
            *[dma((2, stages))] * 2,
            *[dma((panels, PARTS))] * 2,
            *[dma((stages - 1, panels, PARTS))] * 2,
            *[dma((panels, PARTS))] * 2,
        ],
        compiler_params=pltpu.CompilerParams(collective_id=0, has_side_effects=True),
    )(
        panel_vars[None, :], panel_vars, probability[None, :], assignment[:, None],
        barrier, borders[0], kkt_inverse[0], first_section,
    )


def solution(mesh):
    placed = (
        P("scen", None, "row"),
        P("scen", "row", None),
        P("row", None),
        P("row"),
        P(),
        P(),
        P("scen"),
    )
    return jax.shard_map(
        functools.partial(per_device, mesh.shape["scen"], mesh.shape["row"]),
        mesh=mesh, in_specs=placed, out_specs=P("row", None), check_vma=False,
    )
```

```python
import functools

import jax
import jax.numpy as jnp
from jax import lax
from jax.experimental import pallas as pl
from jax.experimental.pallas import tpu as pltpu
from jax.sharding import PartitionSpec as P

PANEL = 128
MESH = pl.DeviceIdType.MESH
HIGH = lax.Precision.HIGHEST
F32 = jnp.float32
BF16 = jnp.bfloat16
PARTS = 3
SUB = 8
BLOCK = 32
MAIN_VMEM = 40 << 20
LAST_VMEM = 8 << 20
STEPS = 32766.0
TINY = 1e-30


def small_factor(tile, first):
    shape = tile.shape
    spread = [
        jnp.broadcast_to(tile[:, first + k:first + k + 1], shape) for k in range(SUB)
    ]
    cell = {
        (i, k): jnp.broadcast_to(spread[k][i:i + 1, :], shape)
        for k in range(SUB) for i in range(k, SUB)
    }
    scale, lower = [], {}
    for j in range(SUB):
        scale.append(lax.rsqrt(cell[j, j]))
        for i in range(j + 1, SUB):
            lower[i, j] = cell[i, j] * scale[j]
        for k in range(j + 1, SUB):
            for i in range(k, SUB):
                cell[i, k] = cell[i, k] - lower[i, j] * lower[k, j]
    inverse = {}
    for j in range(SUB):
        inverse[j, j] = scale[j]
        for i in range(j + 1, SUB):
            total = lower[i, j] * inverse[j, j]
            for m in range(j + 1, i):
                total = total + lower[i, m] * inverse[m, j]
            inverse[i, j] = -(scale[i] * total)
    return inverse


def split2(value):
    high = value.astype(BF16)
    return high, (value - high.astype(F32)).astype(BF16)


def panel_inverse(block, size, hook=None):
    panel = block.shape[0]
    shape = (SUB, panel)
    sub = lax.broadcasted_iota(jnp.int32, shape, 0)
    lane = lax.broadcasted_iota(jnp.int32, shape, 1)
    tiles = panel // SUB
    left = [block[low:low + SUB, :] for low in range(0, panel, SUB)]
    right = [jnp.where(lane == sub + low, 1.0, 0.0) for low in range(0, panel, SUB)]
    per = size // SUB
    for base in range(0, tiles, per):
        for own in range(base, base + per):
            first = own * SUB
            inverse = small_factor(left[own], first)
            new_left = new_right = None
            for k in range(SUB):
                coeff = inverse[SUB - 1, k]
                for i in range(SUB - 2, k - 1, -1):
                    coeff = jnp.where(sub <= i, inverse[i, k], coeff)
                if k:
                    coeff = jnp.where(sub < k, 0.0, coeff)
                add_left = coeff * left[own][k:k + 1, :]
                add_right = coeff * right[own][k:k + 1, :]
                new_left = add_left if k == 0 else new_left + add_left
                new_right = add_right if k == 0 else new_right + add_right
            for tile in range(own + 1, base + per):
                spread = [
                    jnp.broadcast_to(left[tile][:, first + m:first + m + 1], shape)
                    for m in range(SUB)
                ]
                for k in range(SUB):
                    factor = spread[0] * inverse[k, 0]
                    for m in range(1, k + 1):
                        factor = factor + spread[m] * inverse[k, m]
                    left[tile] = left[tile] - factor * new_left[k:k + 1, :]
                    right[tile] = right[tile] - factor * new_right[k:k + 1, :]
            left[own], right[own] = new_left, new_right
        if base + per < tiles:
            upper = jnp.concatenate(left[base:base + per], axis=0)
            both = jnp.concatenate(
                [upper, jnp.concatenate(right[base:base + per], axis=0)], axis=1
            )
            high, low = split2(both)
            change = lax.dot_general(
                jnp.concatenate(
                    [high[:, :panel], high[:, :panel], low[:, :panel]], axis=0
                ),
                jnp.concatenate([high, low, high], axis=0),
                (((0,), (0,)), ((), ())), preferred_element_type=F32,
            )
            for tile in range(base + per, tiles):
                low = tile * SUB
                left[tile] = left[tile] - change[low:low + SUB, :panel]
                right[tile] = right[tile] - change[low:low + SUB, panel:]
        if hook is not None:
            hook(base // per)
    return jnp.concatenate(right, axis=0)


def flip(index, bit):
    return index + bit * (1 - 2 * ((index // bit) % 2))


def toggle(index, mask):
    bit = 1
    while bit <= mask:
        if mask & bit:
            index = flip(index, bit)
        bit *= 2
    return index


def bits_down(count):
    bits = []
    bit = count // 2
    while bit >= 1:
        bits.append(bit)
        bit //= 2
    return bits


def low_bit(mask):
    return mask & -mask


def split3(value):
    high = value.astype(BF16)
    rest = value - high.astype(F32)
    middle = rest.astype(BF16)
    low = (rest - middle.astype(F32)).astype(BF16)
    return high, middle, low


def wide(*mats):
    blocks = []
    for mat in mats:
        high, low = split2(mat)
        blocks.append(jnp.concatenate(
            [jnp.concatenate([high, low], axis=0),
             jnp.concatenate([high, jnp.zeros_like(low)], axis=0)], axis=1))
    return jnp.concatenate(blocks, axis=0)


def product_t(lhs, stacked):
    high, low = split2(lhs)
    both = lax.dot_general(
        jnp.concatenate([high, low], axis=1), stacked, (((1,), (1,)), ((), ())),
        preferred_element_type=F32,
    )
    side = lhs.shape[1]
    return [
        both[:, at:at + side] + both[:, at + side:at + 2 * side]
        for at in range(0, both.shape[1], 2 * side)
    ]


def product(lhs, rhs):
    high, low = split2(lhs)
    top, bottom = split2(rhs)
    both = jnp.dot(
        jnp.concatenate([high, low], axis=1),
        jnp.concatenate(
            [jnp.concatenate([top, bottom], axis=1),
             jnp.concatenate([top, jnp.zeros_like(top)], axis=1)], axis=0),
        preferred_element_type=F32,
    )
    side = rhs.shape[1]
    return both[:, :side] + both[:, side:]


def code(value):
    top = jnp.max(jnp.abs(value), axis=0, keepdims=True)
    unit = jnp.maximum(top, TINY) * (1.0 / STEPS)
    return jnp.round(value * (1.0 / unit)).astype(jnp.int32).astype(jnp.int16), unit


def decode(steps, unit):
    return steps.astype(jnp.int32).astype(F32) * unit


def schur_kernel(
    n_scen, n_row,
    asg, pv_hbm, prob_hbm, bar_hbm, b_hbm, k_hbm, base_hbm,
    left_ref, right_ref, h_ref, stack_ref,
    b_ref, k_ref, base, load_sem, rest_sem, pv_row, pv_s, prob, bar_row, onehot,
    picked, xin, zsum, zin, columns, solved,
    fpick, fxin, fsum, fzin, fall,
    bt, ct, tf, t_sum, t_in,
    first_stack, out_half, in_half, steps, units, steps_in, units_in, h_first,
    rsx_send, rsz_send, ca_send, sa_send, rsz_recv, cx_recv, sx_recv,
    rsx_recv, cz_recv, sz_recv,
    t_send, t_recv, c_send, c_recv, y_send, y_recv, g_send, g_recv,
):
    scen = lax.axis_index("scen")
    row = lax.axis_index("row")
    panels = columns.shape[0]
    depth = columns.shape[2]
    full = n_row * depth
    rows, window = base.shape
    nz = n_row // 2
    z, x = row // 2, row % 2
    other = flip(row, 1)
    barrier = pltpu.get_barrier_semaphore()
    scen_bits = bits_down(n_scen)[::-1]
    y_bits = scen_bits[1:]
    near = [toggle(z, step) for step in range(1, nz)]
    far = near[::-1]
    frow = fpick.shape[1]
    frows = n_row * frow
    groups = window // frows
    fstart = (scen % groups) * frows
    first = row * rows
    done = (h_first, h_ref)

    pl.semaphore_signal(barrier, inc=1, device_id={"row": other}, device_id_type=MESH)
    for peer in far:
        pl.semaphore_signal(
            barrier, inc=1, device_id={"row": 2 * peer + x}, device_id_type=MESH
        )
    for bit in scen_bits:
        pl.semaphore_signal(
            barrier, inc=1, device_id={"scen": flip(scen, bit)}, device_id_type=MESH
        )

    def load(block):
        start = pl.multiple_of(block * depth, depth)
        return pltpu.make_async_copy(
            b_hbm.at[pl.ds(start, depth), :],
            b_ref.at[pl.ds(start, depth), :],
            load_sem.at[block],
        )

    base_load = pltpu.make_async_copy(base_hbm, base, rest_sem.at[0])
    k_load = pltpu.make_async_copy(k_hbm, k_ref, rest_sem.at[1])
    small = [
        pltpu.make_async_copy(source, to, rest_sem.at[2 + index])
        for index, (source, to) in enumerate((
            (pv_hbm, pv_row), (bar_hbm, bar_row), (pv_hbm.at[0], pv_s),
            (prob_hbm, prob),
        ))
    ]
    small[0].start()
    for peer in far + [z]:
        load(2 * peer + 1 - x).start()
    for one in small[1:]:
        one.start()
    base_load.start()
    for peer in far + [z]:
        load(2 * peer + x).start()
    k_load.start()

    small[0].wait()
    onehot[...] = jnp.where(
        lax.broadcasted_iota(jnp.int32, (rows, window), 0) == pv_row[...] - first,
        1.0, 0.0,
    ).astype(BF16)
    pl.semaphore_wait(barrier, nz + len(scen_bits))

    def remote(src, dst, send, recv, where):
        return pltpu.make_async_remote_copy(
            src_ref=src, dst_ref=dst, send_sem=send, recv_sem=recv,
            device_id=where, device_id_type=MESH,
        )

    def go(copy):
        copy.start()

    def drained(held, sem):
        remote(held, held, sem, sem, {"row": other}).wait_send()

    pick_of = [picked.at[p] for p in range(panels)] + [fpick]
    xin_of = [xin.at[p] for p in range(panels)] + [fxin]
    zsum_of = [zsum.at[p] for p in range(panels)] + [fsum]
    zin_of = [zin.at[p] for p in range(panels)] + [fzin]
    col_of = [columns.at[p] for p in range(panels)] + [fall]
    sol_of = [solved.at[p] for p in range(panels)]

    def rsx(p, peer):
        return remote(
            pick_of[p].at[2 * peer + 1 - x], xin_of[p].at[peer],
            rsx_send.at[p], rsx_recv.at[p, peer], {"row": other},
        )

    def rsz_go(p, peer):
        go(remote(
            zsum_of[p].at[peer], zin_of[p].at[z],
            rsz_send.at[p], rsz_recv.at[p], {"row": 2 * peer + x},
        ))

    def rsz_wait(p):
        held = zin_of[p].at[pl.ds(0, nz - 1)]
        remote(held, held, rsz_send.at[p], rsz_recv.at[p], {"row": other}).wait_recv()

    def rs_turn(p):
        for peer in far + [z]:
            rsx(p, peer).wait_recv()
            zsum_of[p][peer] = pick_of[p][2 * peer + x] + xin_of[p][peer]
            if peer is not z:
                rsz_go(p, peer)

    def rs_end(p):
        total = zsum_of[p][z].astype(F32)
        rsz_wait(p)
        for peer in near:
            total = total + zin_of[p][peer].astype(F32)
        col_of[p][row] = total.astype(col_of[p].dtype)

    cols = (col_of, ca_send, cz_recv, cx_recv)
    sols = (sol_of, sa_send, sz_recv, sx_recv)

    def ag_x(kind, p, peer):
        held, send, _, xr = kind
        return remote(
            held[p].at[2 * peer + x], held[p].at[2 * peer + x],
            send.at[p], xr.at[p], {"row": other},
        )

    def ag_start(kind, p):
        held, send, zr, _ = kind
        for peer in far:
            go(remote(
                held[p].at[row], held[p].at[row],
                send.at[p], zr.at[p, z], {"row": 2 * peer + x},
            ))
        go(ag_x(kind, p, z))

    def ag_pass(kind, p, peer):
        held, send, zr, _ = kind
        remote(
            held[p].at[2 * peer + x], held[p].at[2 * peer + x],
            send.at[p], zr.at[p, peer], {"row": 2 * peer + x},
        ).wait_recv()
        go(ag_x(kind, p, peer))

    def ag_end(kind, p):
        held, send, _, xr = kind
        some = held[p].at[pl.ds(0, nz)]
        remote(some, some, send.at[p], xr.at[p], {"row": other}).wait_recv()

    def pick(dst):
        load(dst).wait()
        start = pl.multiple_of(dst * depth, depth)
        block = jnp.dot(
            b_ref[pl.ds(start, depth), :], onehot[...], preferred_element_type=F32
        ).astype(BF16)
        for p in range(panels):
            picked[p, dst] = block[:, p * PANEL:(p + 1) * PANEL]

    for peer in far + [z]:
        pick(2 * peer + 1 - x)
        go(rsx(0, peer))
    for p in range(1, panels):
        for peer in far + [z]:
            go(rsx(p, peer))
    for one in small[1:]:
        one.wait()
    bar = split3(bar_row[...].reshape(1, rows))
    level = lax.broadcasted_iota(jnp.int32, (2 * SUB, rows), 0)
    bars = jnp.where(
        level == 0, bar[0].astype(F32),
        jnp.where(level == 1, bar[1].astype(F32),
                  jnp.where(level == 2, bar[2].astype(F32), 0.0)),
    ).astype(BF16)

    bsel = jnp.sum(
        jnp.dot(bars, onehot[...], preferred_element_type=F32), axis=0, keepdims=True
    )
    base_load.wait()
    slot_row = lax.broadcasted_iota(jnp.int32, (frow, window), 0) + fstart
    slot_col = lax.broadcasted_iota(jnp.int32, (frow, window), 1)

    def frag(block, carry):
        lines = []
        for i in range(frow):
            at = pv_s[fstart + block * frow + i] - first
            inside = jnp.logical_and(at >= 0, at < rows)
            line = base[pl.ds(jnp.clip(at, 0, rows - 1), 1), :]
            lines.append(jnp.where(inside, line, 0.0))
        fpick[block] = jnp.concatenate(lines, axis=0) + jnp.where(
            slot_row + block * frow == slot_col, bsel, 0.0
        )
        return carry

    lax.fori_loop(0, n_row, frag, 0)
    for peer in far + [z]:
        go(rsx(panels, peer))

    for peer in far + [z]:
        pick(2 * peer + x)

    for p in range(panels):
        rs_turn(p)

    def turn(tile, carry):
        start = pl.multiple_of(tile * PANEL, PANEL)
        bt[pl.ds(start, PANEL), :] = b_ref[:, pl.ds(start, PANEL)].T
        return carry

    def solve(p):
        solved[p, row] = jnp.dot(
            k_ref[...], columns[p].reshape(full, PANEL), preferred_element_type=F32
        ).astype(BF16)

    def side(p):
        ct[p] = columns[p].reshape(full, PANEL).T

    rs_end(0)
    ag_start(cols, 0)
    base[...] += onehot[...].astype(F32) * bsel
    tiles = rows // PANEL
    lax.fori_loop(0, tiles // 2, turn, 0)
    ag_pass(cols, 0, near[0])
    rs_end(1)
    ag_start(cols, 1)
    rs_turn(panels)
    for peer in near[1:]:
        ag_pass(cols, 0, peer)
    ag_pass(cols, 1, near[0])
    lax.fori_loop(tiles // 2, tiles, turn, 0)
    k_load.wait()
    ag_end(cols, 0)
    solve(0)
    ag_start(sols, 0)
    rs_end(panels)
    ag_start(cols, panels)
    for peer in near[1:]:
        ag_pass(cols, 1, peer)
    side(0)
    ag_pass(sols, 0, near[0])
    ag_end(cols, 1)
    solve(1)
    ag_start(sols, 1)
    for peer in near:
        ag_pass(cols, panels, peer)
    for peer in near[1:]:
        ag_pass(sols, 0, peer)
    side(1)
    for peer in near[:-1]:
        ag_pass(sols, 1, peer)
    ag_end(cols, panels)
    tf[...] = jnp.zeros_like(tf)
    keep = jnp.where(scen < groups, 1.0, 0.0)
    tf[pl.ds(pl.multiple_of(fstart, SUB), frows), :] = fall[...].reshape(frows, window) * keep
    weight = prob[asg[0]]

    def t_block(p, q):
        return weight * jnp.dot(
            ct[p], solved[q].reshape(full, PANEL), preferred_element_type=F32
        ) + tf[p * PANEL:(p + 1) * PANEL, q * PANEL:(q + 1) * PANEL]

    spans = [pl.ds(0, PANEL), pl.ds(PANEL, 2 * PANEL)]

    def t_copy(which, index):
        return remote(
            t_sum.at[index, spans[which]], t_in.at[index, spans[which]],
            t_send.at[which, index], t_recv.at[which, index],
            {"scen": flip(scen, scen_bits[index])},
        )

    def t_step(which, index):
        t_copy(which, index).wait_recv()
        t_sum[index + 1, spans[which]] = (
            t_sum[index, spans[which]] + t_in[index, spans[which]]
        )
        if index + 1 < len(scen_bits):
            go(t_copy(which, index + 1))

    core = scen % 2
    half = rows // 2
    chunk = half // PARTS
    parts = range(PARTS)

    def place(which, part):
        return pl.ds(pl.multiple_of(which * half + part * chunk, SUB), chunk)

    def term(which, p, part):
        return weight * jnp.dot(
            bt[place(which, part), :], solved[p].reshape(full, PANEL),
            preferred_element_type=F32,
        )

    def c_copy(p, part):
        return remote(
            out_half.at[p, part], in_half.at[p, part],
            c_send.at[0], c_recv.at[p, part], {"scen": flip(scen, 1)},
        )

    def y_copies(index, p, part):
        where = {"scen": flip(scen, y_bits[index])}
        return (
            remote(
                steps.at[index, p, part], steps_in.at[index, p, part],
                y_send.at[0], y_recv.at[0, index, p, part], where,
            ),
            remote(
                units.at[index, p, part], units_in.at[index, p, part],
                y_send.at[1], y_recv.at[1, index, p, part], where,
            ),
        )

    def y_start(index, p, part, value):
        steps[index, p, part], unit = code(value)
        units[index, p, part] = jnp.broadcast_to(unit, units.shape[3:])
        for one in y_copies(index, p, part):
            go(one)

    def g_copy(p, part, which):
        return remote(
            done[p].at[place(which, part), :], done[p].at[place(which, part), :],
            g_send.at[p], g_recv.at[p], {"scen": flip(scen, 1)},
        )

    def h_out(p):
        for part in parts:
            out_half[p, part] = term(1 - core, p, part)
            go(c_copy(p, part))

    def h_join(p, part):
        own = term(core, p, part)
        c_copy(p, part).wait_recv()
        y_start(0, p, part, own + in_half[p, part])

    def y_step(p, part):
        for index in range(len(y_bits)):
            for one in y_copies(index, p, part):
                one.wait_recv()
            total = decode(
                steps[index, p, part], units[index, p, part][0:1, :]
            ) + decode(steps_in[index, p, part], units_in[index, p, part][0:1, :])
            if index + 1 < len(y_bits):
                y_start(index + 1, p, part, total)
            else:
                done[p][place(core, part), :] = (
                    total + base[place(core, part), p * PANEL:(p + 1) * PANEL]
                )
                go(g_copy(p, part, core))

    ag_end(sols, 0)
    whole = t_block(0, 0)
    t_sum[0, spans[0]] = 0.5 * (whole + whole.T)
    go(t_copy(0, 0))
    for peer in near[-1:]:
        ag_pass(sols, 1, peer)
    t_step(0, 0)
    h_out(0)
    h_join(0, 0)
    ag_end(sols, 1)
    t_sum[0, PANEL:2 * PANEL] = 0.5 * (t_block(1, 0) + t_block(0, 1).T)
    whole = t_block(1, 1)
    t_sum[0, 2 * PANEL:] = 0.5 * (whole + whole.T)
    go(t_copy(1, 0))
    for index in range(1, len(scen_bits)):
        t_step(0, index)
    last = len(scen_bits)

    def hook_0(stage):
        if stage == 0:
            t_step(1, 0)
            for part in parts[1:]:
                h_join(0, part)
        elif stage == 1:
            h_out(1)
        elif stage == 2:
            for part in parts:
                h_join(1, part)

    inverse_0 = panel_inverse(t_sum[last, spans[0]], BLOCK, hook_0)
    for index in range(1, len(scen_bits)):
        t_step(1, index)
    lower = product_t(t_sum[last, PANEL:2 * PANEL], wide(inverse_0))[0]
    block = t_sum[last, 2 * PANEL:] - product_t(lower, wide(lower))[0]

    def g_end(p):
        some = done[p].at[pl.ds(0, half), :]
        remote(
            some, some, g_send.at[p], g_recv.at[p], {"scen": flip(scen, 1)}
        ).wait_recv()

    def drop(which, part):
        left, right = product_t(h_first[place(which, part), :], first_stack[...])
        left_ref[place(which, part), :] = left
        right_ref[place(which, part), :] = right

    def hook(stage):
        if stage == 0:
            first_stack[...] = wide(inverse_0, product(lower, inverse_0))
            for part in parts:
                y_step(0, part)
        elif stage == 1:
            g_end(0)
            for part in parts:
                drop(core, part)
        elif stage == 2:
            for part in parts:
                y_step(1, part)
            for part in parts:
                drop(1 - core, part)

    stack_ref[...] = wide(panel_inverse(block, BLOCK, hook))
    g_end(1)
    for p in range(panels + 1):
        drained(xin_of[p], rsx_send.at[p])
        drained(zin_of[p].at[pl.ds(0, nz - 1)], rsz_send.at[p])
        drained(col_of[p].at[pl.ds(0, n_row - 1)], ca_send.at[p])
    for p in range(panels):
        drained(sol_of[p].at[pl.ds(0, n_row - 1)], sa_send.at[p])
        drained(done[p].at[pl.ds(0, half), :], g_send.at[p])
    for which in range(2):
        for index in range(len(scen_bits)):
            t_copy(which, index).wait_send()
    drained(out_half, c_send.at[0])
    drained(steps, y_send.at[0])
    drained(units, y_send.at[1])


def last_kernel(pieces, left_ref, right_ref, h_ref, stack_ref, out_hbm, out, sem):
    size = out.shape[0] // pieces

    def store(side, piece, source):
        return pltpu.make_async_copy(
            source.at[pl.ds(piece * size, size), :],
            out_hbm.at[pl.ds(piece * size, size), pl.ds(side * PANEL, PANEL)],
            sem.at[side, piece],
        )

    for piece in range(pieces):
        store(0, piece, left_ref).start()
    for piece in range(pieces):
        span = pl.ds(piece * size, size)
        out[span, :] = product_t(h_ref[span, :] - right_ref[span, :], stack_ref[...])[0]
        store(1, piece, out).start()
    for piece in range(pieces):
        store(0, piece, left_ref).wait()
        store(1, piece, out).wait()


def per_device(
    n_scen, n_row,
    borders, kkt_inverse, first_section, barrier, panel_vars, probability, assignment,
):
    rows, window = first_section.shape
    depth = kkt_inverse.shape[1]
    full = kkt_inverse.shape[2]
    panels = window // PANEL
    nz = n_row // 2
    groups = max(1, min(n_scen, window // (8 * n_row)))
    frow = window // groups // n_row
    stages = n_scen.bit_length() - 1
    chunk = rows // 2 // PARTS
    dma = pltpu.SemaphoreType.DMA
    vmem = pl.BlockSpec(memory_space=pltpu.VMEM)

    def buf(shape, dtype):
        return pltpu.VMEM(shape, dtype)

    held = pl.pallas_call(
        functools.partial(schur_kernel, n_scen, n_row),
        out_shape=(
            buf((rows, PANEL), F32), buf((rows, PANEL), F32), buf((rows, PANEL), F32),
            buf((2 * PANEL, 2 * PANEL), BF16),
        ),
        in_specs=[pl.BlockSpec(memory_space=pltpu.SMEM)]
        + [pl.BlockSpec(memory_space=pltpu.HBM)] * 6,
        out_specs=(vmem,) * 4,
        scratch_shapes=[
            buf((full, rows), BF16), buf((depth, full), BF16), buf((rows, window), F32),
            dma((n_row,)), dma((6,)),
            buf((1, window), jnp.int32), pltpu.SMEM((window,), jnp.int32),
            pltpu.SMEM((n_scen,), F32), buf((rows,), F32),
            buf((rows, window), BF16),
            buf((panels, n_row, depth, PANEL), BF16),
            buf((panels, nz, depth, PANEL), BF16),
            buf((panels, nz, depth, PANEL), BF16),
            buf((panels, nz, depth, PANEL), BF16),
            buf((panels, n_row, depth, PANEL), BF16),
            buf((panels, n_row, depth, PANEL), BF16),
            buf((n_row, frow, window), F32),
            buf((nz, frow, window), F32),
            buf((nz, frow, window), F32),
            buf((nz, frow, window), F32),
            buf((n_row, frow, window), F32),
            buf((rows, full), BF16), buf((panels, PANEL, full), BF16),
            buf((window, window), F32),
            buf((stages + 1, 3 * PANEL, PANEL), F32),
            buf((stages, 3 * PANEL, PANEL), F32),
            buf((4 * PANEL, 2 * PANEL), BF16),
            buf((panels, PARTS, chunk, PANEL), F32),
            buf((panels, PARTS, chunk, PANEL), F32),
            *[buf((stages - 1, panels, PARTS, chunk, PANEL), jnp.int16),
              buf((stages - 1, panels, PARTS, SUB, PANEL), F32)] * 2,
            buf((rows, PANEL), F32),
            *[dma((panels + 1,))] * 3, dma((panels,)), *[dma((panels + 1,))] * 2,
            dma((panels,)), *[dma((panels + 1, nz))] * 2, dma((panels, nz)),
            *[dma((2, stages))] * 2,
            dma((1,)), dma((panels, PARTS)),
            dma((2,)), dma((2, stages - 1, panels, PARTS)),
            *[dma((panels,))] * 2,
        ],
        compiler_params=pltpu.CompilerParams(
            collective_id=0, has_side_effects=True, vmem_limit_bytes=MAIN_VMEM
        ),
    )(
        assignment,
        *[pltpu.with_memory_space_constraint(one, pltpu.HBM)
          for one in (panel_vars[None, :], probability, barrier,
                      borders[0], kkt_inverse[0], first_section)],
    )
    pieces = 2 * PARTS
    return pl.pallas_call(
        functools.partial(last_kernel, pieces),
        out_shape=jax.ShapeDtypeStruct((rows, window), F32),
        in_specs=[vmem] * 4,
        out_specs=pl.BlockSpec(memory_space=pl.ANY),
        scratch_shapes=[buf((rows, PANEL), F32), dma((2, pieces))],
        compiler_params=pltpu.CompilerParams(vmem_limit_bytes=LAST_VMEM),
    )(*[pltpu.with_memory_space_constraint(one, pltpu.VMEM) for one in held])


def solution(mesh):
    placed = (
        P("scen", None, "row"),
        P("scen", "row", None),
        P("row", None),
        P("row"),
        P(),
        P(),
        P("scen"),
    )
    return jax.shard_map(
        functools.partial(per_device, mesh.shape["scen"], mesh.shape["row"]),
        mesh=mesh, in_specs=placed, out_specs=P("row", None), check_vma=False,
    )
```

```python
import functools

import jax
import jax.numpy as jnp
from jax import lax
from jax.experimental import pallas as pl
from jax.experimental.pallas import tpu as pltpu
from jax.sharding import PartitionSpec as P

PANEL = 128
MESH = pl.DeviceIdType.MESH
HIGH = lax.Precision.HIGHEST
F32 = jnp.float32
BF16 = jnp.bfloat16
PARTS = 3
SUB = 8
BLOCK = 32
MAIN_VMEM = 40 << 20
LAST_VMEM = 8 << 20
STEPS = 32766.0
TINY = 1e-30


def small_factor(tile, first):
    shape = tile.shape
    spread = [
        jnp.broadcast_to(tile[:, first + k:first + k + 1], shape) for k in range(SUB)
    ]
    cell = {
        (i, k): jnp.broadcast_to(spread[k][i:i + 1, :], shape)
        for k in range(SUB) for i in range(k, SUB)
    }
    scale, lower = [], {}
    for j in range(SUB):
        scale.append(lax.rsqrt(cell[j, j]))
        for i in range(j + 1, SUB):
            lower[i, j] = cell[i, j] * scale[j]
        for k in range(j + 1, SUB):
            for i in range(k, SUB):
                cell[i, k] = cell[i, k] - lower[i, j] * lower[k, j]
    inverse = {}
    for j in range(SUB):
        inverse[j, j] = scale[j]
        for i in range(j + 1, SUB):
            total = lower[i, j] * inverse[j, j]
            for m in range(j + 1, i):
                total = total + lower[i, m] * inverse[m, j]
            inverse[i, j] = -(scale[i] * total)
    return inverse


def split2(value):
    high = value.astype(BF16)
    return high, (value - high.astype(F32)).astype(BF16)


def panel_inverse(block, size, hook=None):
    panel = block.shape[0]
    shape = (SUB, panel)
    sub = lax.broadcasted_iota(jnp.int32, shape, 0)
    lane = lax.broadcasted_iota(jnp.int32, shape, 1)
    tiles = panel // SUB
    left = [block[low:low + SUB, :] for low in range(0, panel, SUB)]
    right = [jnp.where(lane == sub + low, 1.0, 0.0) for low in range(0, panel, SUB)]
    per = size // SUB
    for base in range(0, tiles, per):
        for own in range(base, base + per):
            first = own * SUB
            inverse = small_factor(left[own], first)
            new_left = new_right = None
            for k in range(SUB):
                coeff = inverse[SUB - 1, k]
                for i in range(SUB - 2, k - 1, -1):
                    coeff = jnp.where(sub <= i, inverse[i, k], coeff)
                if k:
                    coeff = jnp.where(sub < k, 0.0, coeff)
                add_left = coeff * left[own][k:k + 1, :]
                add_right = coeff * right[own][k:k + 1, :]
                new_left = add_left if k == 0 else new_left + add_left
                new_right = add_right if k == 0 else new_right + add_right
            for tile in range(own + 1, base + per):
                spread = [
                    jnp.broadcast_to(left[tile][:, first + m:first + m + 1], shape)
                    for m in range(SUB)
                ]
                for k in range(SUB):
                    factor = spread[0] * inverse[k, 0]
                    for m in range(1, k + 1):
                        factor = factor + spread[m] * inverse[k, m]
                    left[tile] = left[tile] - factor * new_left[k:k + 1, :]
                    right[tile] = right[tile] - factor * new_right[k:k + 1, :]
            left[own], right[own] = new_left, new_right
            if hook is not None:
                hook(own)
        if base + per < tiles:
            upper = jnp.concatenate(left[base:base + per], axis=0)
            both = jnp.concatenate(
                [upper, jnp.concatenate(right[base:base + per], axis=0)], axis=1
            )
            high, low = split2(both)
            change = lax.dot_general(
                jnp.concatenate(
                    [high[:, :panel], high[:, :panel], low[:, :panel]], axis=0
                ),
                jnp.concatenate([high, low, high], axis=0),
                (((0,), (0,)), ((), ())), preferred_element_type=F32,
            )
            for tile in range(base + per, tiles):
                low = tile * SUB
                left[tile] = left[tile] - change[low:low + SUB, :panel]
                right[tile] = right[tile] - change[low:low + SUB, panel:]
    return jnp.concatenate(right, axis=0)


def flip(index, bit):
    return index + bit * (1 - 2 * ((index // bit) % 2))


def toggle(index, mask):
    bit = 1
    while bit <= mask:
        if mask & bit:
            index = flip(index, bit)
        bit *= 2
    return index


def bits_down(count):
    bits = []
    bit = count // 2
    while bit >= 1:
        bits.append(bit)
        bit //= 2
    return bits


def low_bit(mask):
    return mask & -mask


def split3(value):
    high = value.astype(BF16)
    rest = value - high.astype(F32)
    middle = rest.astype(BF16)
    low = (rest - middle.astype(F32)).astype(BF16)
    return high, middle, low


def wide(*mats):
    blocks = []
    for mat in mats:
        high, low = split2(mat)
        blocks.append(jnp.concatenate(
            [jnp.concatenate([high, low], axis=0),
             jnp.concatenate([high, jnp.zeros_like(low)], axis=0)], axis=1))
    return jnp.concatenate(blocks, axis=0)


def product_t(lhs, stacked):
    high, low = split2(lhs)
    both = lax.dot_general(
        jnp.concatenate([high, low], axis=1), stacked, (((1,), (1,)), ((), ())),
        preferred_element_type=F32,
    )
    side = lhs.shape[1]
    return [
        both[:, at:at + side] + both[:, at + side:at + 2 * side]
        for at in range(0, both.shape[1], 2 * side)
    ]


def product(lhs, rhs):
    high, low = split2(lhs)
    top, bottom = split2(rhs)
    both = jnp.dot(
        jnp.concatenate([high, low], axis=1),
        jnp.concatenate(
            [jnp.concatenate([top, bottom], axis=1),
             jnp.concatenate([top, jnp.zeros_like(top)], axis=1)], axis=0),
        preferred_element_type=F32,
    )
    side = rhs.shape[1]
    return both[:, :side] + both[:, side:]


def code(value):
    top = jnp.max(jnp.abs(value), axis=0, keepdims=True)
    unit = jnp.maximum(top, TINY) * (1.0 / STEPS)
    return jnp.round(value * (1.0 / unit)).astype(jnp.int32).astype(jnp.int16), unit


def decode(steps, unit):
    return steps.astype(jnp.int32).astype(F32) * unit


def schur_kernel(
    n_scen, n_row,
    asg, pv_hbm, prob_hbm, bar_hbm, b_hbm, k_hbm, base_hbm,
    left_ref, right_ref, h_ref, stack_ref,
    b_ref, k_ref, base, load_sem, rest_sem, pv_row, pv_s, prob, bar_row, onehot,
    picked, xin, zsum, zin, columns, solved,
    fpick, fxin, fsum, fzin, fall,
    bt, ct, tf, t_sum, t_in, u_own, u_in, u_sum, u_all, mine,
    first_stack, out_half, in_half, steps, units, steps_in, units_in, h_first,
    rsx_send, rsz_send, ca_send, sa_send, rsz_recv, cx_recv, sx_recv,
    rsx_recv, cz_recv, sz_recv,
    t_send, t_recv, u_send, u_recv, c_send, c_recv, y_send, y_recv, g_send, g_recv,
):
    scen = lax.axis_index("scen")
    row = lax.axis_index("row")
    panels = columns.shape[0]
    depth = columns.shape[2]
    full = n_row * depth
    rows, window = base.shape
    nz = n_row // 2
    z, x = row // 2, row % 2
    other = flip(row, 1)
    barrier = pltpu.get_barrier_semaphore()
    scen_bits = bits_down(n_scen)[::-1]
    y_bits = scen_bits[1:]
    near = [toggle(z, step) for step in range(1, nz)]
    far = near[::-1]
    frow = fpick.shape[1]
    frows = n_row * frow
    groups = window // frows
    fstart = (scen % groups) * frows
    first = row * rows
    done = (h_first, h_ref)

    pl.semaphore_signal(barrier, inc=1, device_id={"row": other}, device_id_type=MESH)
    for peer in far:
        pl.semaphore_signal(
            barrier, inc=1, device_id={"row": 2 * peer + x}, device_id_type=MESH
        )
    for bit in scen_bits:
        pl.semaphore_signal(
            barrier, inc=1, device_id={"scen": flip(scen, bit)}, device_id_type=MESH
        )

    def load(block):
        start = pl.multiple_of(block * depth, depth)
        return pltpu.make_async_copy(
            b_hbm.at[pl.ds(start, depth), :],
            b_ref.at[pl.ds(start, depth), :],
            load_sem.at[block],
        )

    base_load = pltpu.make_async_copy(base_hbm, base, rest_sem.at[0])
    k_load = pltpu.make_async_copy(k_hbm, k_ref, rest_sem.at[1])
    small = [
        pltpu.make_async_copy(source, to, rest_sem.at[2 + index])
        for index, (source, to) in enumerate((
            (pv_hbm, pv_row), (bar_hbm, bar_row), (pv_hbm.at[0], pv_s),
            (prob_hbm, prob),
        ))
    ]
    small[0].start()
    for peer in far + [z]:
        load(2 * peer + 1 - x).start()
    for one in small[1:]:
        one.start()
    base_load.start()
    for peer in far + [z]:
        load(2 * peer + x).start()
    k_load.start()

    small[0].wait()
    onehot[...] = jnp.where(
        lax.broadcasted_iota(jnp.int32, (rows, window), 0) == pv_row[...] - first,
        1.0, 0.0,
    ).astype(BF16)
    pl.semaphore_wait(barrier, nz + len(scen_bits))

    def remote(src, dst, send, recv, where):
        return pltpu.make_async_remote_copy(
            src_ref=src, dst_ref=dst, send_sem=send, recv_sem=recv,
            device_id=where, device_id_type=MESH,
        )

    def go(copy):
        copy.start()

    def drained(held, sem):
        remote(held, held, sem, sem, {"row": other}).wait_send()

    pick_of = [picked.at[p] for p in range(panels)] + [fpick]
    xin_of = [xin.at[p] for p in range(panels)] + [fxin]
    zsum_of = [zsum.at[p] for p in range(panels)] + [fsum]
    zin_of = [zin.at[p] for p in range(panels)] + [fzin]
    col_of = [columns.at[p] for p in range(panels)] + [fall]
    sol_of = [solved.at[p] for p in range(panels)]

    def rsx(p, peer):
        return remote(
            pick_of[p].at[2 * peer + 1 - x], xin_of[p].at[peer],
            rsx_send.at[p], rsx_recv.at[p, peer], {"row": other},
        )

    def rsz_go(p, peer):
        go(remote(
            zsum_of[p].at[peer], zin_of[p].at[z],
            rsz_send.at[p], rsz_recv.at[p], {"row": 2 * peer + x},
        ))

    def rsz_wait(p):
        held = zin_of[p].at[pl.ds(0, nz - 1)]
        remote(held, held, rsz_send.at[p], rsz_recv.at[p], {"row": other}).wait_recv()

    def rs_turn(p):
        for peer in far + [z]:
            rsx(p, peer).wait_recv()
            zsum_of[p][peer] = pick_of[p][2 * peer + x] + xin_of[p][peer]
            if peer is not z:
                rsz_go(p, peer)

    def rs_end(p):
        total = zsum_of[p][z].astype(F32)
        rsz_wait(p)
        for peer in near:
            total = total + zin_of[p][peer].astype(F32)
        col_of[p][row] = total.astype(col_of[p].dtype)

    cols = (col_of, ca_send, cz_recv, cx_recv)
    sols = (sol_of, sa_send, sz_recv, sx_recv)

    def ag_x(kind, p, peer):
        held, send, _, xr = kind
        return remote(
            held[p].at[2 * peer + x], held[p].at[2 * peer + x],
            send.at[p], xr.at[p], {"row": other},
        )

    def ag_start(kind, p):
        held, send, zr, _ = kind
        for peer in near:
            go(remote(
                held[p].at[row], held[p].at[row],
                send.at[p], zr.at[p, z], {"row": 2 * peer + x},
            ))
        go(ag_x(kind, p, z))

    def ag_pass(kind, p, peer):
        held, send, zr, _ = kind
        remote(
            held[p].at[2 * peer + x], held[p].at[2 * peer + x],
            send.at[p], zr.at[p, peer], {"row": 2 * peer + x},
        ).wait_recv()
        go(ag_x(kind, p, peer))

    def ag_end(kind, p):
        held, send, _, xr = kind
        some = held[p].at[pl.ds(0, nz)]
        remote(some, some, send.at[p], xr.at[p], {"row": other}).wait_recv()

    def pick(dst):
        load(dst).wait()
        start = pl.multiple_of(dst * depth, depth)
        block = jnp.dot(
            b_ref[pl.ds(start, depth), :], onehot[...], preferred_element_type=F32
        ).astype(BF16)
        for p in range(panels):
            picked[p, dst] = block[:, p * PANEL:(p + 1) * PANEL]

    for peer in far + [z]:
        pick(2 * peer + 1 - x)
        go(rsx(0, peer))
    for p in range(1, panels):
        for peer in far + [z]:
            go(rsx(p, peer))
    for one in small[1:]:
        one.wait()
    bar = split3(bar_row[...].reshape(1, rows))
    level = lax.broadcasted_iota(jnp.int32, (2 * SUB, rows), 0)
    bars = jnp.where(
        level == 0, bar[0].astype(F32),
        jnp.where(level == 1, bar[1].astype(F32),
                  jnp.where(level == 2, bar[2].astype(F32), 0.0)),
    ).astype(BF16)

    bsel = jnp.sum(
        jnp.dot(bars, onehot[...], preferred_element_type=F32), axis=0, keepdims=True
    )
    base_load.wait()
    slot_row = lax.broadcasted_iota(jnp.int32, (frow, window), 0) + fstart
    slot_col = lax.broadcasted_iota(jnp.int32, (frow, window), 1)

    def frag(block, carry):
        lines = []
        for i in range(frow):
            at = pv_s[fstart + block * frow + i] - first
            inside = jnp.logical_and(at >= 0, at < rows)
            line = base[pl.ds(jnp.clip(at, 0, rows - 1), 1), :]
            lines.append(jnp.where(inside, line, 0.0))
        fpick[block] = jnp.concatenate(lines, axis=0) + jnp.where(
            slot_row + block * frow == slot_col, bsel, 0.0
        )
        return carry

    lax.fori_loop(0, n_row, frag, 0)
    for peer in far + [z]:
        go(rsx(panels, peer))

    for peer in far + [z]:
        pick(2 * peer + x)

    for p in range(panels):
        rs_turn(p)

    def turn(tile, carry):
        start = pl.multiple_of(tile * PANEL, PANEL)
        bt[pl.ds(start, PANEL), :] = b_ref[:, pl.ds(start, PANEL)].T
        return carry

    def solve(p):
        solved[p, row] = jnp.dot(
            k_ref[...], columns[p].reshape(full, PANEL), preferred_element_type=F32
        ).astype(BF16)

    def side(p):
        ct[p] = columns[p].reshape(full, PANEL).T

    rs_end(0)
    ag_start(cols, 0)
    base[...] += onehot[...].astype(F32) * bsel
    tiles = rows // PANEL
    lax.fori_loop(0, tiles // 2, turn, 0)
    ag_pass(cols, 0, near[0])
    rs_end(1)
    ag_start(cols, 1)
    rs_turn(panels)
    for peer in near[1:]:
        ag_pass(cols, 0, peer)
    ag_pass(cols, 1, near[0])
    lax.fori_loop(tiles // 2, tiles, turn, 0)
    k_load.wait()
    ag_end(cols, 0)
    solve(0)
    ag_start(sols, 0)
    rs_end(panels)
    ag_start(cols, panels)
    for peer in near[1:]:
        ag_pass(cols, 1, peer)
    side(0)
    ag_pass(sols, 0, near[0])
    ag_end(cols, 1)
    solve(1)
    ag_start(sols, 1)
    for peer in near:
        ag_pass(cols, panels, peer)
    for peer in near[1:]:
        ag_pass(sols, 0, peer)
    side(1)
    for peer in near[:-1]:
        ag_pass(sols, 1, peer)
    ag_end(cols, panels)
    tf[...] = jnp.zeros_like(tf)
    keep = jnp.where(scen < groups, 1.0, 0.0)
    tf[pl.ds(pl.multiple_of(fstart, SUB), frows), :] = fall[...].reshape(frows, window) * keep
    weight = prob[asg[0]]

    def t_block(p, q):
        return weight * jnp.dot(
            ct[p], solved[q].reshape(full, PANEL), preferred_element_type=F32
        ) + tf[p * PANEL:(p + 1) * PANEL, q * PANEL:(q + 1) * PANEL]

    core = scen % 2
    pair = {"scen": flip(scen, 1)}
    bits = range(len(scen_bits))

    def shared(own, into, sums, total, send, recv):
        size = own.shape[0] // 2
        here = pl.ds(pl.multiple_of(core * size, SUB), size)
        there = pl.ds(pl.multiple_of((1 - core) * size, SUB), size)
        final = len(scen_bits)

        def copy(index):
            return remote(
                own.at[there, :] if index == 0 else sums.at[index - 1],
                total.at[here, :] if index == final else into.at[index],
                send.at[index], recv.at[index],
                {"scen": flip(scen, scen_bits[index % final])},
            )

        def step(index):
            copy(index).wait_recv()
            before = own[here, :] if index == 0 else sums[index - 1]
            sums[index] = before + into[index]
            go(copy(index + 1))
            if index + 1 == final:
                total[here, :] = sums[index]

        def end():
            remote(
                sums.at[0], total.at[there, :], send.at[final], recv.at[final], pair
            ).wait_recv()

        return copy, step, end

    def t_copy(index):
        return remote(
            t_sum.at[index], t_in.at[index], t_send.at[index], t_recv.at[index],
            {"scen": flip(scen, scen_bits[index])},
        )

    def t_step(index):
        t_copy(index).wait_recv()
        t_sum[index + 1] = t_sum[index] + t_in[index]
        if index + 1 < len(scen_bits):
            go(t_copy(index + 1))

    u_copy, u_step, u_end = shared(u_own, u_in, u_sum, u_all, u_send, u_recv)

    half = rows // 2
    chunk = half // PARTS
    parts = range(PARTS)

    def place(which, part):
        return pl.ds(pl.multiple_of(which * half + part * chunk, SUB), chunk)

    def term(which, p, part):
        return weight * jnp.dot(
            bt[place(which, part), :], solved[p].reshape(full, PANEL),
            preferred_element_type=F32,
        )

    def c_copy(p, part):
        return remote(
            out_half.at[p, part], in_half.at[p, part],
            c_send.at[0], c_recv.at[p, part], {"scen": flip(scen, 1)},
        )

    def y_copies(index, p, part):
        where = {"scen": flip(scen, y_bits[index])}
        return (
            remote(
                steps.at[index, p, part], steps_in.at[index, p, part],
                y_send.at[0], y_recv.at[0, index, p, part], where,
            ),
            remote(
                units.at[index, p, part], units_in.at[index, p, part],
                y_send.at[1], y_recv.at[1, index, p, part], where,
            ),
        )

    def y_code(index, p, part, value):
        steps[index, p, part], unit = code(value)
        units[index, p, part] = jnp.broadcast_to(unit, units.shape[3:])

    def y_go(index, p, part):
        for one in y_copies(index, p, part):
            go(one)

    def g_copy(p, part, which):
        return remote(
            done[p].at[place(which, part), :], done[p].at[place(which, part), :],
            g_send.at[p], g_recv.at[p], {"scen": flip(scen, 1)},
        )

    def h_out(p):
        for part in parts:
            out_half[p, part] = term(1 - core, p, part)

    def h_own(p):
        for part in parts:
            mine[part] = term(core, p, part)

    def c_go(p):
        for part in parts:
            go(c_copy(p, part))

    def h_join(p, part):
        y_code(0, p, part, mine[part] + in_half[p, part])

    def y_wait(p, part):
        for index in range(len(y_bits)):
            for one in y_copies(index, p, part):
                one.wait_recv()
            if index + 1 < len(y_bits):
                y_code(index + 1, p, part, y_total(index, p, part))
                y_go(index + 1, p, part)

    def y_total(index, p, part):
        return decode(
            steps[index, p, part], units[index, p, part][0:1, :]
        ) + decode(steps_in[index, p, part], units_in[index, p, part][0:1, :])

    def h_end(p, part):
        done[p][place(core, part), :] = (
            y_total(len(y_bits) - 1, p, part)
            + base[place(core, part), p * PANEL:(p + 1) * PANEL]
        )

    ag_end(sols, 0)
    whole = t_block(0, 0)
    t_sum[0] = 0.5 * (whole + whole.T)
    go(t_copy(0))
    for peer in near[-1:]:
        ag_pass(sols, 1, peer)
    t_step(0)
    h_out(0)
    c_go(0)
    h_own(0)
    for part in parts[:2]:
        c_copy(0, part).wait_recv()
        h_join(0, part)
        y_go(0, 0, part)
    for part in parts[2:]:
        c_copy(0, part).wait_recv()
        h_join(0, part)
    ag_end(sols, 1)
    u_own[:PANEL, :] = 0.5 * (t_block(1, 0) + t_block(0, 1).T)
    whole = t_block(1, 1)
    u_own[PANEL:, :] = 0.5 * (whole + whole.T)
    go(u_copy(0))
    for index in bits[1:]:
        t_step(index)

    def hook_0(tile):
        if tile == 1:
            u_step(0)
            for part in parts[2:]:
                y_go(0, 0, part)
            h_out(1)
        elif tile == 4:
            c_go(1)
            h_own(1)
        elif tile == 8:
            for part in parts:
                c_copy(1, part).wait_recv()
            for part in parts:
                h_join(1, part)
        elif tile == 11:
            for part in parts:
                y_go(0, 1, part)
        elif tile == 14:
            for index in bits[1:]:
                u_step(index)

    inverse_0 = panel_inverse(t_sum[len(scen_bits)], BLOCK, hook_0)
    for part in parts[:2]:
        y_wait(0, part)
        h_end(0, part)
        go(g_copy(0, part, core))
    u_end()
    lower = product_t(u_all[:PANEL, :], wide(inverse_0))[0]
    block = u_all[PANEL:, :] - product_t(lower, wide(lower))[0]

    def g_end(p):
        some = done[p].at[pl.ds(0, half), :]
        remote(some, some, g_send.at[p], g_recv.at[p], pair).wait_recv()

    def drop(which, part):
        left, right = product_t(h_first[place(which, part), :], first_stack[...])
        left_ref[place(which, part), :] = left
        right_ref[place(which, part), :] = right

    def hook(tile):
        if tile == 0:
            first_stack[...] = wide(inverse_0, product(lower, inverse_0))
        elif tile == 2:
            for part in parts[2:]:
                y_wait(0, part)
            for part in parts[2:]:
                h_end(0, part)
        elif tile == 4:
            for part in parts[2:]:
                go(g_copy(0, part, core))
            for part in parts:
                drop(core, part)
        elif tile == 8:
            g_end(0)
            for part in parts:
                drop(1 - core, part)
        elif tile == 11:
            for part in parts[:2]:
                y_wait(1, part)
            for part in parts[:2]:
                h_end(1, part)
        elif tile == 13:
            for part in parts[:2]:
                go(g_copy(1, part, core))
            for part in parts[2:]:
                y_wait(1, part)
            for part in parts[2:]:
                h_end(1, part)
        elif tile == 14:
            for part in parts[2:]:
                go(g_copy(1, part, core))

    stack_ref[...] = wide(panel_inverse(block, BLOCK, hook))
    g_end(1)
    for p in range(panels + 1):
        drained(xin_of[p], rsx_send.at[p])
        drained(zin_of[p].at[pl.ds(0, nz - 1)], rsz_send.at[p])
        drained(col_of[p].at[pl.ds(0, n_row - 1)], ca_send.at[p])
    for p in range(panels):
        drained(sol_of[p].at[pl.ds(0, n_row - 1)], sa_send.at[p])
        drained(done[p].at[pl.ds(0, half), :], g_send.at[p])
    for index in bits:
        t_copy(index).wait_send()
    for index in range(len(scen_bits) + 1):
        u_copy(index).wait_send()
    drained(out_half, c_send.at[0])
    drained(steps, y_send.at[0])
    drained(units, y_send.at[1])


def last_kernel(pieces, left_ref, right_ref, h_ref, stack_ref, out_hbm, out, sem):
    size = out.shape[0] // pieces

    def store(side, piece, source):
        return pltpu.make_async_copy(
            source.at[pl.ds(piece * size, size), :],
            out_hbm.at[pl.ds(piece * size, size), pl.ds(side * PANEL, PANEL)],
            sem.at[side, piece],
        )

    for piece in range(pieces):
        store(0, piece, left_ref).start()
    for piece in range(pieces):
        span = pl.ds(piece * size, size)
        out[span, :] = product_t(h_ref[span, :] - right_ref[span, :], stack_ref[...])[0]
        store(1, piece, out).start()
    for piece in range(pieces):
        store(0, piece, left_ref).wait()
        store(1, piece, out).wait()


def per_device(
    n_scen, n_row,
    borders, kkt_inverse, first_section, barrier, panel_vars, probability, assignment,
):
    rows, window = first_section.shape
    depth = kkt_inverse.shape[1]
    full = kkt_inverse.shape[2]
    panels = window // PANEL
    nz = n_row // 2
    groups = max(1, min(n_scen, window // (8 * n_row)))
    frow = window // groups // n_row
    stages = n_scen.bit_length() - 1
    chunk = rows // 2 // PARTS
    dma = pltpu.SemaphoreType.DMA
    vmem = pl.BlockSpec(memory_space=pltpu.VMEM)

    def buf(shape, dtype):
        return pltpu.VMEM(shape, dtype)

    held = pl.pallas_call(
        functools.partial(schur_kernel, n_scen, n_row),
        out_shape=(
            buf((rows, PANEL), F32), buf((rows, PANEL), F32), buf((rows, PANEL), F32),
            buf((2 * PANEL, 2 * PANEL), BF16),
        ),
        in_specs=[pl.BlockSpec(memory_space=pltpu.SMEM)]
        + [pl.BlockSpec(memory_space=pltpu.HBM)] * 6,
        out_specs=(vmem,) * 4,
        scratch_shapes=[
            buf((full, rows), BF16), buf((depth, full), BF16), buf((rows, window), F32),
            dma((n_row,)), dma((6,)),
            buf((1, window), jnp.int32), pltpu.SMEM((window,), jnp.int32),
            pltpu.SMEM((n_scen,), F32), buf((rows,), F32),
            buf((rows, window), BF16),
            buf((panels, n_row, depth, PANEL), BF16),
            buf((panels, nz, depth, PANEL), BF16),
            buf((panels, nz, depth, PANEL), BF16),
            buf((panels, nz, depth, PANEL), BF16),
            buf((panels, n_row, depth, PANEL), BF16),
            buf((panels, n_row, depth, PANEL), BF16),
            buf((n_row, frow, window), F32),
            buf((nz, frow, window), F32),
            buf((nz, frow, window), F32),
            buf((nz, frow, window), F32),
            buf((n_row, frow, window), F32),
            buf((rows, full), BF16), buf((panels, PANEL, full), BF16),
            buf((window, window), F32),
            buf((stages + 1, PANEL, PANEL), F32), buf((stages, PANEL, PANEL), F32),
            buf((2 * PANEL, PANEL), F32), buf((stages, PANEL, PANEL), F32),
            buf((stages, PANEL, PANEL), F32), buf((2 * PANEL, PANEL), F32),
            buf((PARTS, chunk, PANEL), F32),
            buf((4 * PANEL, 2 * PANEL), BF16),
            buf((panels, PARTS, chunk, PANEL), F32),
            buf((panels, PARTS, chunk, PANEL), F32),
            *[buf((stages - 1, panels, PARTS, chunk, PANEL), jnp.int16),
              buf((stages - 1, panels, PARTS, SUB, PANEL), F32)] * 2,
            buf((rows, PANEL), F32),
            *[dma((panels + 1,))] * 3, dma((panels,)), *[dma((panels + 1,))] * 2,
            dma((panels,)), *[dma((panels + 1, nz))] * 2, dma((panels, nz)),
            *[dma((stages,))] * 2, *[dma((stages + 1,))] * 2,
            dma((1,)), dma((panels, PARTS)),
            dma((2,)), dma((2, stages - 1, panels, PARTS)),
            *[dma((panels,))] * 2,
        ],
        compiler_params=pltpu.CompilerParams(
            collective_id=0, has_side_effects=True, vmem_limit_bytes=MAIN_VMEM
        ),
    )(
        assignment,
        *[pltpu.with_memory_space_constraint(one, pltpu.HBM)
          for one in (panel_vars[None, :], probability, barrier,
                      borders[0], kkt_inverse[0], first_section)],
    )
    pieces = 2 * PARTS
    return pl.pallas_call(
        functools.partial(last_kernel, pieces),
        out_shape=jax.ShapeDtypeStruct((rows, window), F32),
        in_specs=[vmem] * 4,
        out_specs=pl.BlockSpec(memory_space=pl.ANY),
        scratch_shapes=[buf((rows, PANEL), F32), dma((2, pieces))],
        compiler_params=pltpu.CompilerParams(vmem_limit_bytes=LAST_VMEM),
    )(*[pltpu.with_memory_space_constraint(one, pltpu.VMEM) for one in held])


def solution(mesh):
    placed = (
        P("scen", None, "row"),
        P("scen", "row", None),
        P("row", None),
        P("row"),
        P(),
        P(),
        P("scen"),
    )
    return jax.shard_map(
        functools.partial(per_device, mesh.shape["scen"], mesh.shape["row"]),
        mesh=mesh, in_specs=placed, out_specs=P("row", None), check_vma=False,
    )
```

```python
import functools

import jax
import jax.numpy as jnp
from jax import lax
from jax.experimental import pallas as pl
from jax.experimental.pallas import tpu as pltpu
from jax.sharding import PartitionSpec as P

PANEL = 128
MESH = pl.DeviceIdType.MESH
HIGH = lax.Precision.HIGHEST
F32 = jnp.float32
BF16 = jnp.bfloat16
PARTS = 3
SUB = 8
BLOCK = 32
MAIN_VMEM = 40 << 20
LAST_VMEM = 8 << 20
STEPS = 32766.0
TINY = 1e-30


def small_factor(spread):
    shape = spread[0].shape
    cell = {
        (i, k): jnp.broadcast_to(spread[k][i:i + 1, :], shape)
        for k in range(SUB) for i in range(k, SUB)
    }
    scale, lower = [], {}
    for j in range(SUB):
        scale.append(lax.rsqrt(cell[j, j]))
        for i in range(j + 1, SUB):
            lower[i, j] = cell[i, j] * scale[j]
        for k in range(j + 1, SUB):
            for i in range(k, SUB):
                cell[i, k] = cell[i, k] - lower[i, j] * lower[k, j]
    inverse = {}
    for j in range(SUB):
        inverse[j, j] = scale[j]
        for i in range(j + 1, SUB):
            total = lower[i, j] * inverse[j, j]
            for m in range(j + 1, i):
                total = total + lower[i, m] * inverse[m, j]
            inverse[i, j] = -(scale[i] * total)
    return inverse


def split2(value):
    high = value.astype(BF16)
    return high, (value - high.astype(F32)).astype(BF16)


def panel_inverse(block, size, hook=None):
    panel = block.shape[0]
    shape = (SUB, panel)
    sub = lax.broadcasted_iota(jnp.int32, shape, 0)
    lane = lax.broadcasted_iota(jnp.int32, shape, 1)
    tiles = panel // SUB
    left = [block[low:low + SUB, :] for low in range(0, panel, SUB)]
    right = [jnp.where(lane == sub + low, 1.0, 0.0) for low in range(0, panel, SUB)]
    per = size // SUB
    for base in range(0, tiles, per):
        spread = {
            (tile, own): [
                jnp.broadcast_to(left[tile][:, at:at + 1], shape)
                for at in range(own * SUB, own * SUB + SUB)
            ]
            for tile in range(base, base + per) for own in range(base, tile + 1)
        }
        for own in range(base, base + per):
            inverse = small_factor(spread[own, own])
            rest = range(own + 1, base + per)
            factors, lines = {}, {}
            for tile in rest:
                column = spread[tile, own]
                for k in range(SUB):
                    factor = column[0] * inverse[k, 0]
                    for m in range(1, k + 1):
                        factor = factor + column[m] * inverse[k, m]
                    factors[tile, k] = factor
                    for i in range(SUB):
                        lines[tile, k, i] = jnp.broadcast_to(factor[i:i + 1, :], shape)
                for across in range(own + 1, tile + 1):
                    for i in range(SUB):
                        change = factors[tile, 0] * lines[across, 0, i]
                        for k in range(1, SUB):
                            change = change + factors[tile, k] * lines[across, k, i]
                        spread[tile, across][i] = spread[tile, across][i] - change
            new_left = new_right = None
            for k in range(SUB):
                coeff = inverse[SUB - 1, k]
                for i in range(SUB - 2, k - 1, -1):
                    coeff = jnp.where(sub <= i, inverse[i, k], coeff)
                if k:
                    coeff = jnp.where(sub < k, 0.0, coeff)
                add_left = coeff * left[own][k:k + 1, :]
                add_right = coeff * right[own][k:k + 1, :]
                new_left = add_left if k == 0 else new_left + add_left
                new_right = add_right if k == 0 else new_right + add_right
            for tile in rest:
                for k in range(SUB):
                    left[tile] = left[tile] - factors[tile, k] * new_left[k:k + 1, :]
                    right[tile] = right[tile] - factors[tile, k] * new_right[k:k + 1, :]
            left[own], right[own] = new_left, new_right
            if hook is not None:
                hook(own)
        if base + per < tiles:
            upper = jnp.concatenate(left[base:base + per], axis=0)
            both = jnp.concatenate(
                [upper, jnp.concatenate(right[base:base + per], axis=0)], axis=1
            )
            high, low = split2(both)
            change = lax.dot_general(
                jnp.concatenate(
                    [high[:, :panel], high[:, :panel], low[:, :panel]], axis=0
                ),
                jnp.concatenate([high, low, high], axis=0),
                (((0,), (0,)), ((), ())), preferred_element_type=F32,
            )
            for tile in range(base + per, tiles):
                low = tile * SUB
                left[tile] = left[tile] - change[low:low + SUB, :panel]
                right[tile] = right[tile] - change[low:low + SUB, panel:]
    return jnp.concatenate(right, axis=0)


def flip(index, bit):
    return index + bit * (1 - 2 * ((index // bit) % 2))


def toggle(index, mask):
    bit = 1
    while bit <= mask:
        if mask & bit:
            index = flip(index, bit)
        bit *= 2
    return index


def bits_down(count):
    bits = []
    bit = count // 2
    while bit >= 1:
        bits.append(bit)
        bit //= 2
    return bits


def low_bit(mask):
    return mask & -mask


def split3(value):
    high = value.astype(BF16)
    rest = value - high.astype(F32)
    middle = rest.astype(BF16)
    low = (rest - middle.astype(F32)).astype(BF16)
    return high, middle, low


def wide(*mats):
    blocks = []
    for mat in mats:
        high, low = split2(mat)
        blocks.append(jnp.concatenate(
            [jnp.concatenate([high, low], axis=0),
             jnp.concatenate([high, jnp.zeros_like(low)], axis=0)], axis=1))
    return jnp.concatenate(blocks, axis=0)


def product_t(lhs, stacked):
    high, low = split2(lhs)
    both = lax.dot_general(
        jnp.concatenate([high, low], axis=1), stacked, (((1,), (1,)), ((), ())),
        preferred_element_type=F32,
    )
    side = lhs.shape[1]
    return [
        both[:, at:at + side] + both[:, at + side:at + 2 * side]
        for at in range(0, both.shape[1], 2 * side)
    ]


def product(lhs, rhs):
    high, low = split2(lhs)
    top, bottom = split2(rhs)
    both = jnp.dot(
        jnp.concatenate([high, low], axis=1),
        jnp.concatenate(
            [jnp.concatenate([top, bottom], axis=1),
             jnp.concatenate([top, jnp.zeros_like(top)], axis=1)], axis=0),
        preferred_element_type=F32,
    )
    side = rhs.shape[1]
    return both[:, :side] + both[:, side:]


def code(value):
    top = jnp.max(jnp.abs(value), axis=0, keepdims=True)
    unit = jnp.maximum(top, TINY) * (1.0 / STEPS)
    return jnp.round(value * (1.0 / unit)).astype(jnp.int32).astype(jnp.int16), unit


def decode(steps, unit):
    return steps.astype(jnp.int32).astype(F32) * unit


def schur_kernel(
    n_scen, n_row,
    asg, pv_hbm, prob_hbm, bar_hbm, b_hbm, k_hbm, base_hbm,
    left_ref, right_ref, h_ref, stack_ref,
    b_ref, k_ref, base, load_sem, rest_sem, pv_row, pv_s, prob, bar_row, onehot,
    picked, xin, zsum, zin, columns, solved,
    fpick, fxin, fsum, fzin, fall,
    bt, ct, tf, t_sum, t_in, u_own, u_in, u_sum, u_all, mine,
    first_stack, out_half, in_half, steps, units, steps_in, units_in, h_first,
    rsx_send, rsz_send, ca_send, sa_send, rsz_recv, cx_recv, sx_recv,
    rsx_recv, cz_recv, sz_recv,
    t_send, t_recv, u_send, u_recv, c_send, c_recv, y_send, y_recv, g_send, g_recv,
):
    scen = lax.axis_index("scen")
    row = lax.axis_index("row")
    panels = columns.shape[0]
    depth = columns.shape[2]
    full = n_row * depth
    rows, window = base.shape
    nz = n_row // 2
    z, x = row // 2, row % 2
    other = flip(row, 1)
    barrier = pltpu.get_barrier_semaphore()
    scen_bits = bits_down(n_scen)[::-1]
    y_bits = scen_bits[1:]
    near = [toggle(z, step) for step in range(1, nz)]
    far = near[::-1]
    frow = fpick.shape[1]
    frows = n_row * frow
    groups = window // frows
    fstart = (scen % groups) * frows
    first = row * rows
    done = (h_first, h_ref)

    pl.semaphore_signal(barrier, inc=1, device_id={"row": other}, device_id_type=MESH)
    for peer in far:
        pl.semaphore_signal(
            barrier, inc=1, device_id={"row": 2 * peer + x}, device_id_type=MESH
        )
    for bit in scen_bits:
        pl.semaphore_signal(
            barrier, inc=1, device_id={"scen": flip(scen, bit)}, device_id_type=MESH
        )

    def load(block):
        start = pl.multiple_of(block * depth, depth)
        return pltpu.make_async_copy(
            b_hbm.at[pl.ds(start, depth), :],
            b_ref.at[pl.ds(start, depth), :],
            load_sem.at[block],
        )

    base_load = pltpu.make_async_copy(base_hbm, base, rest_sem.at[0])
    k_load = pltpu.make_async_copy(k_hbm, k_ref, rest_sem.at[1])
    small = [
        pltpu.make_async_copy(source, to, rest_sem.at[2 + index])
        for index, (source, to) in enumerate((
            (pv_hbm, pv_row), (bar_hbm, bar_row), (pv_hbm.at[0], pv_s),
            (prob_hbm, prob),
        ))
    ]
    small[0].start()
    for peer in far + [z]:
        load(2 * peer + 1 - x).start()
    for one in small[1:]:
        one.start()
    base_load.start()
    for peer in far + [z]:
        load(2 * peer + x).start()
    k_load.start()

    small[0].wait()
    onehot[...] = jnp.where(
        lax.broadcasted_iota(jnp.int32, (rows, window), 0) == pv_row[...] - first,
        1.0, 0.0,
    ).astype(BF16)
    pl.semaphore_wait(barrier, nz + len(scen_bits))

    def remote(src, dst, send, recv, where):
        return pltpu.make_async_remote_copy(
            src_ref=src, dst_ref=dst, send_sem=send, recv_sem=recv,
            device_id=where, device_id_type=MESH,
        )

    def go(copy):
        copy.start()

    def drained(held, sem):
        remote(held, held, sem, sem, {"row": other}).wait_send()

    pick_of = [picked.at[p] for p in range(panels)] + [fpick]
    xin_of = [xin.at[p] for p in range(panels)] + [fxin]
    zsum_of = [zsum.at[p] for p in range(panels)] + [fsum]
    zin_of = [zin.at[p] for p in range(panels)] + [fzin]
    col_of = [columns.at[p] for p in range(panels)] + [fall]
    sol_of = [solved.at[p] for p in range(panels)]

    def rsx(p, peer):
        return remote(
            pick_of[p].at[2 * peer + 1 - x], xin_of[p].at[peer],
            rsx_send.at[p], rsx_recv.at[p, peer], {"row": other},
        )

    def rsz_go(p, peer):
        go(remote(
            zsum_of[p].at[peer], zin_of[p].at[z],
            rsz_send.at[p], rsz_recv.at[p], {"row": 2 * peer + x},
        ))

    def rsz_wait(p):
        held = zin_of[p].at[pl.ds(0, nz - 1)]
        remote(held, held, rsz_send.at[p], rsz_recv.at[p], {"row": other}).wait_recv()

    def rs_turn(p):
        for peer in far + [z]:
            rsx(p, peer).wait_recv()
            zsum_of[p][peer] = pick_of[p][2 * peer + x] + xin_of[p][peer]
            if peer is not z:
                rsz_go(p, peer)

    def rs_end(p):
        total = zsum_of[p][z].astype(F32)
        rsz_wait(p)
        for peer in near:
            total = total + zin_of[p][peer].astype(F32)
        col_of[p][row] = total.astype(col_of[p].dtype)

    cols = (col_of, ca_send, cz_recv, cx_recv)
    sols = (sol_of, sa_send, sz_recv, sx_recv)

    def ag_x(kind, p, peer):
        held, send, _, xr = kind
        return remote(
            held[p].at[2 * peer + x], held[p].at[2 * peer + x],
            send.at[p], xr.at[p], {"row": other},
        )

    def ag_start(kind, p):
        held, send, zr, _ = kind
        for peer in near:
            go(remote(
                held[p].at[row], held[p].at[row],
                send.at[p], zr.at[p, z], {"row": 2 * peer + x},
            ))
        go(ag_x(kind, p, z))

    def ag_pass(kind, p, peer):
        held, send, zr, _ = kind
        remote(
            held[p].at[2 * peer + x], held[p].at[2 * peer + x],
            send.at[p], zr.at[p, peer], {"row": 2 * peer + x},
        ).wait_recv()
        go(ag_x(kind, p, peer))

    def ag_end(kind, p):
        held, send, _, xr = kind
        some = held[p].at[pl.ds(0, nz)]
        remote(some, some, send.at[p], xr.at[p], {"row": other}).wait_recv()

    def pick(dst):
        load(dst).wait()
        start = pl.multiple_of(dst * depth, depth)
        block = jnp.dot(
            b_ref[pl.ds(start, depth), :], onehot[...], preferred_element_type=F32
        ).astype(BF16)
        for p in range(panels):
            picked[p, dst] = block[:, p * PANEL:(p + 1) * PANEL]

    for peer in far + [z]:
        pick(2 * peer + 1 - x)
        go(rsx(0, peer))
    for p in range(1, panels):
        for peer in far + [z]:
            go(rsx(p, peer))
    for one in small[1:]:
        one.wait()
    bar = split3(bar_row[...].reshape(1, rows))
    level = lax.broadcasted_iota(jnp.int32, (2 * SUB, rows), 0)
    bars = jnp.where(
        level == 0, bar[0].astype(F32),
        jnp.where(level == 1, bar[1].astype(F32),
                  jnp.where(level == 2, bar[2].astype(F32), 0.0)),
    ).astype(BF16)

    bsel = jnp.sum(
        jnp.dot(bars, onehot[...], preferred_element_type=F32), axis=0, keepdims=True
    )
    base_load.wait()
    slot_row = lax.broadcasted_iota(jnp.int32, (frow, window), 0) + fstart
    slot_col = lax.broadcasted_iota(jnp.int32, (frow, window), 1)

    def frag(block, carry):
        lines = []
        for i in range(frow):
            at = pv_s[fstart + block * frow + i] - first
            inside = jnp.logical_and(at >= 0, at < rows)
            line = base[pl.ds(jnp.clip(at, 0, rows - 1), 1), :]
            lines.append(jnp.where(inside, line, 0.0))
        fpick[block] = jnp.concatenate(lines, axis=0) + jnp.where(
            slot_row + block * frow == slot_col, bsel, 0.0
        )
        return carry

    lax.fori_loop(0, n_row, frag, 0)
    for peer in far + [z]:
        go(rsx(panels, peer))

    for peer in far + [z]:
        pick(2 * peer + x)

    for p in range(panels):
        rs_turn(p)

    def turn(tile, carry):
        start = pl.multiple_of(tile * PANEL, PANEL)
        bt[pl.ds(start, PANEL), :] = b_ref[:, pl.ds(start, PANEL)].T
        return carry

    def solve(p):
        solved[p, row] = jnp.dot(
            k_ref[...], columns[p].reshape(full, PANEL), preferred_element_type=F32
        ).astype(BF16)

    def side(p):
        ct[p] = columns[p].reshape(full, PANEL).T

    rs_end(0)
    ag_start(cols, 0)
    base[...] += onehot[...].astype(F32) * bsel
    tiles = rows // PANEL
    lax.fori_loop(0, tiles // 2, turn, 0)
    ag_pass(cols, 0, near[0])
    rs_end(1)
    ag_start(cols, 1)
    rs_turn(panels)
    for peer in near[1:]:
        ag_pass(cols, 0, peer)
    ag_pass(cols, 1, near[0])
    lax.fori_loop(tiles // 2, tiles, turn, 0)
    k_load.wait()
    ag_end(cols, 0)
    solve(0)
    ag_start(sols, 0)
    rs_end(panels)
    ag_start(cols, panels)
    for peer in near[1:]:
        ag_pass(cols, 1, peer)
    side(0)
    ag_pass(sols, 0, near[0])
    ag_end(cols, 1)
    solve(1)
    ag_start(sols, 1)
    for peer in near:
        ag_pass(cols, panels, peer)
    for peer in near[1:]:
        ag_pass(sols, 0, peer)
    side(1)
    for peer in near[:-1]:
        ag_pass(sols, 1, peer)
    ag_end(cols, panels)
    tf[...] = jnp.zeros_like(tf)
    keep = jnp.where(scen < groups, 1.0, 0.0)
    tf[pl.ds(pl.multiple_of(fstart, SUB), frows), :] = fall[...].reshape(frows, window) * keep
    weight = prob[asg[0]]

    def t_block(p, q):
        return weight * jnp.dot(
            ct[p], solved[q].reshape(full, PANEL), preferred_element_type=F32
        ) + tf[p * PANEL:(p + 1) * PANEL, q * PANEL:(q + 1) * PANEL]

    core = scen % 2
    pair = {"scen": flip(scen, 1)}
    bits = range(len(scen_bits))

    def shared(own, into, sums, total, send, recv):
        size = own.shape[0] // 2
        here = pl.ds(pl.multiple_of(core * size, SUB), size)
        there = pl.ds(pl.multiple_of((1 - core) * size, SUB), size)
        final = len(scen_bits)

        def copy(index):
            return remote(
                own.at[there, :] if index == 0 else sums.at[index - 1],
                total.at[here, :] if index == final else into.at[index],
                send.at[index], recv.at[index],
                {"scen": flip(scen, scen_bits[index % final])},
            )

        def step(index):
            copy(index).wait_recv()
            before = own[here, :] if index == 0 else sums[index - 1]
            sums[index] = before + into[index]
            go(copy(index + 1))
            if index + 1 == final:
                total[here, :] = sums[index]

        def end():
            remote(
                sums.at[0], total.at[there, :], send.at[final], recv.at[final], pair
            ).wait_recv()

        return copy, step, end

    def t_copy(index):
        return remote(
            t_sum.at[index], t_in.at[index], t_send.at[index], t_recv.at[index],
            {"scen": flip(scen, scen_bits[index])},
        )

    def t_step(index):
        t_copy(index).wait_recv()
        t_sum[index + 1] = t_sum[index] + t_in[index]
        if index + 1 < len(scen_bits):
            go(t_copy(index + 1))

    u_copy, u_step, u_end = shared(u_own, u_in, u_sum, u_all, u_send, u_recv)

    half = rows // 2
    chunk = half // PARTS
    parts = range(PARTS)

    def place(which, part):
        return pl.ds(pl.multiple_of(which * half + part * chunk, SUB), chunk)

    def term(which, p, part):
        return weight * jnp.dot(
            bt[place(which, part), :], solved[p].reshape(full, PANEL),
            preferred_element_type=F32,
        )

    def c_copy(p, part):
        return remote(
            out_half.at[p, part], in_half.at[p, part],
            c_send.at[0], c_recv.at[p, part], {"scen": flip(scen, 1)},
        )

    def y_copies(index, p, part):
        where = {"scen": flip(scen, y_bits[index])}
        return (
            remote(
                steps.at[index, p, part], steps_in.at[index, p, part],
                y_send.at[0], y_recv.at[0, index, p, part], where,
            ),
            remote(
                units.at[index, p, part], units_in.at[index, p, part],
                y_send.at[1], y_recv.at[1, index, p, part], where,
            ),
        )

    def y_code(index, p, part, value):
        steps[index, p, part], unit = code(value)
        units[index, p, part] = jnp.broadcast_to(unit, units.shape[3:])

    def y_go(index, p, part):
        for one in y_copies(index, p, part):
            go(one)

    def g_copy(p, part, which):
        return remote(
            done[p].at[place(which, part), :], done[p].at[place(which, part), :],
            g_send.at[p], g_recv.at[p], {"scen": flip(scen, 1)},
        )

    def h_out(p):
        for part in parts:
            out_half[p, part] = term(1 - core, p, part)

    def h_own(p):
        for part in parts:
            mine[part] = term(core, p, part)

    def c_go(p):
        for part in parts:
            go(c_copy(p, part))

    def h_join(p, part):
        y_code(0, p, part, mine[part] + in_half[p, part])

    def y_wait(p, part):
        for index in range(len(y_bits)):
            for one in y_copies(index, p, part):
                one.wait_recv()
            if index + 1 < len(y_bits):
                y_code(index + 1, p, part, y_total(index, p, part))
                y_go(index + 1, p, part)

    def y_total(index, p, part):
        return decode(
            steps[index, p, part], units[index, p, part][0:1, :]
        ) + decode(steps_in[index, p, part], units_in[index, p, part][0:1, :])

    def h_end(p, part):
        done[p][place(core, part), :] = (
            y_total(len(y_bits) - 1, p, part)
            + base[place(core, part), p * PANEL:(p + 1) * PANEL]
        )

    ag_end(sols, 0)
    whole = t_block(0, 0)
    t_sum[0] = 0.5 * (whole + whole.T)
    go(t_copy(0))
    for peer in near[-1:]:
        ag_pass(sols, 1, peer)
    t_step(0)
    h_out(0)
    c_go(0)
    h_own(0)
    for part in parts[:2]:
        c_copy(0, part).wait_recv()
        h_join(0, part)
        y_go(0, 0, part)
    for part in parts[2:]:
        c_copy(0, part).wait_recv()
        h_join(0, part)
    ag_end(sols, 1)
    u_own[:PANEL, :] = 0.5 * (t_block(1, 0) + t_block(0, 1).T)
    whole = t_block(1, 1)
    u_own[PANEL:, :] = 0.5 * (whole + whole.T)
    go(u_copy(0))
    for index in bits[1:]:
        t_step(index)

    def hook_0(tile):
        if tile == 1:
            u_step(0)
            for part in parts[2:]:
                y_go(0, 0, part)
            h_out(1)
        elif tile == 4:
            c_go(1)
            h_own(1)
        elif tile == 8:
            for part in parts:
                c_copy(1, part).wait_recv()
            for part in parts:
                h_join(1, part)
        elif tile == 11:
            for part in parts:
                y_go(0, 1, part)
        elif tile == 14:
            for index in bits[1:]:
                u_step(index)

    inverse_0 = panel_inverse(t_sum[len(scen_bits)], BLOCK, hook_0)
    for part in parts[:2]:
        y_wait(0, part)
        h_end(0, part)
        go(g_copy(0, part, core))
    u_end()
    lower = product_t(u_all[:PANEL, :], wide(inverse_0))[0]
    block = u_all[PANEL:, :] - product_t(lower, wide(lower))[0]

    def g_end(p):
        some = done[p].at[pl.ds(0, half), :]
        remote(some, some, g_send.at[p], g_recv.at[p], pair).wait_recv()

    def drop(which, part):
        left, right = product_t(h_first[place(which, part), :], first_stack[...])
        left_ref[place(which, part), :] = left
        right_ref[place(which, part), :] = right

    def hook(tile):
        if tile == 0:
            first_stack[...] = wide(inverse_0, product(lower, inverse_0))
        elif tile == 2:
            for part in parts[2:]:
                y_wait(0, part)
            for part in parts[2:]:
                h_end(0, part)
        elif tile == 4:
            for part in parts[2:]:
                go(g_copy(0, part, core))
            for part in parts:
                drop(core, part)
        elif tile == 8:
            g_end(0)
            for part in parts:
                drop(1 - core, part)
        elif tile == 11:
            for part in parts[:2]:
                y_wait(1, part)
            for part in parts[:2]:
                h_end(1, part)
        elif tile == 13:
            for part in parts[:2]:
                go(g_copy(1, part, core))
            for part in parts[2:]:
                y_wait(1, part)
            for part in parts[2:]:
                h_end(1, part)
        elif tile == 14:
            for part in parts[2:]:
                go(g_copy(1, part, core))

    stack_ref[...] = wide(panel_inverse(block, BLOCK, hook))
    g_end(1)
    for p in range(panels + 1):
        drained(xin_of[p], rsx_send.at[p])
        drained(zin_of[p].at[pl.ds(0, nz - 1)], rsz_send.at[p])
        drained(col_of[p].at[pl.ds(0, n_row - 1)], ca_send.at[p])
    for p in range(panels):
        drained(sol_of[p].at[pl.ds(0, n_row - 1)], sa_send.at[p])
        drained(done[p].at[pl.ds(0, half), :], g_send.at[p])
    for index in bits:
        t_copy(index).wait_send()
    for index in range(len(scen_bits) + 1):
        u_copy(index).wait_send()
    drained(out_half, c_send.at[0])
    drained(steps, y_send.at[0])
    drained(units, y_send.at[1])


def last_kernel(pieces, left_ref, right_ref, h_ref, stack_ref, out_hbm, out, sem):
    size = out.shape[0] // pieces

    def store(side, piece, source):
        return pltpu.make_async_copy(
            source.at[pl.ds(piece * size, size), :],
            out_hbm.at[pl.ds(piece * size, size), pl.ds(side * PANEL, PANEL)],
            sem.at[side, piece],
        )

    for piece in range(pieces):
        store(0, piece, left_ref).start()
    for piece in range(pieces):
        span = pl.ds(piece * size, size)
        out[span, :] = product_t(h_ref[span, :] - right_ref[span, :], stack_ref[...])[0]
        store(1, piece, out).start()
    for piece in range(pieces):
        store(0, piece, left_ref).wait()
        store(1, piece, out).wait()


def per_device(
    n_scen, n_row,
    borders, kkt_inverse, first_section, barrier, panel_vars, probability, assignment,
):
    rows, window = first_section.shape
    depth = kkt_inverse.shape[1]
    full = kkt_inverse.shape[2]
    panels = window // PANEL
    nz = n_row // 2
    groups = max(1, min(n_scen, window // (8 * n_row)))
    frow = window // groups // n_row
    stages = n_scen.bit_length() - 1
    chunk = rows // 2 // PARTS
    dma = pltpu.SemaphoreType.DMA
    vmem = pl.BlockSpec(memory_space=pltpu.VMEM)

    def buf(shape, dtype):
        return pltpu.VMEM(shape, dtype)

    held = pl.pallas_call(
        functools.partial(schur_kernel, n_scen, n_row),
        out_shape=(
            buf((rows, PANEL), F32), buf((rows, PANEL), F32), buf((rows, PANEL), F32),
            buf((2 * PANEL, 2 * PANEL), BF16),
        ),
        in_specs=[pl.BlockSpec(memory_space=pltpu.SMEM)]
        + [pl.BlockSpec(memory_space=pltpu.HBM)] * 6,
        out_specs=(vmem,) * 4,
        scratch_shapes=[
            buf((full, rows), BF16), buf((depth, full), BF16), buf((rows, window), F32),
            dma((n_row,)), dma((6,)),
            buf((1, window), jnp.int32), pltpu.SMEM((window,), jnp.int32),
            pltpu.SMEM((n_scen,), F32), buf((rows,), F32),
            buf((rows, window), BF16),
            buf((panels, n_row, depth, PANEL), BF16),
            buf((panels, nz, depth, PANEL), BF16),
            buf((panels, nz, depth, PANEL), BF16),
            buf((panels, nz, depth, PANEL), BF16),
            buf((panels, n_row, depth, PANEL), BF16),
            buf((panels, n_row, depth, PANEL), BF16),
            buf((n_row, frow, window), F32),
            buf((nz, frow, window), F32),
            buf((nz, frow, window), F32),
            buf((nz, frow, window), F32),
            buf((n_row, frow, window), F32),
            buf((rows, full), BF16), buf((panels, PANEL, full), BF16),
            buf((window, window), F32),
            buf((stages + 1, PANEL, PANEL), F32), buf((stages, PANEL, PANEL), F32),
            buf((2 * PANEL, PANEL), F32), buf((stages, PANEL, PANEL), F32),
            buf((stages, PANEL, PANEL), F32), buf((2 * PANEL, PANEL), F32),
            buf((PARTS, chunk, PANEL), F32),
            buf((4 * PANEL, 2 * PANEL), BF16),
            buf((panels, PARTS, chunk, PANEL), F32),
            buf((panels, PARTS, chunk, PANEL), F32),
            *[buf((stages - 1, panels, PARTS, chunk, PANEL), jnp.int16),
              buf((stages - 1, panels, PARTS, SUB, PANEL), F32)] * 2,
            buf((rows, PANEL), F32),
            *[dma((panels + 1,))] * 3, dma((panels,)), *[dma((panels + 1,))] * 2,
            dma((panels,)), *[dma((panels + 1, nz))] * 2, dma((panels, nz)),
            *[dma((stages,))] * 2, *[dma((stages + 1,))] * 2,
            dma((1,)), dma((panels, PARTS)),
            dma((2,)), dma((2, stages - 1, panels, PARTS)),
            *[dma((panels,))] * 2,
        ],
        compiler_params=pltpu.CompilerParams(
            collective_id=0, has_side_effects=True, vmem_limit_bytes=MAIN_VMEM
        ),
    )(
        assignment,
        *[pltpu.with_memory_space_constraint(one, pltpu.HBM)
          for one in (panel_vars[None, :], probability, barrier,
                      borders[0], kkt_inverse[0], first_section)],
    )
    pieces = 2 * PARTS
    return pl.pallas_call(
        functools.partial(last_kernel, pieces),
        out_shape=jax.ShapeDtypeStruct((rows, window), F32),
        in_specs=[vmem] * 4,
        out_specs=pl.BlockSpec(memory_space=pl.ANY),
        scratch_shapes=[buf((rows, PANEL), F32), dma((2, pieces))],
        compiler_params=pltpu.CompilerParams(vmem_limit_bytes=LAST_VMEM),
    )(*[pltpu.with_memory_space_constraint(one, pltpu.VMEM) for one in held])


def solution(mesh):
    placed = (
        P("scen", None, "row"),
        P("scen", "row", None),
        P("row", None),
        P("row"),
        P(),
        P(),
        P("scen"),
    )
    return jax.shard_map(
        functools.partial(per_device, mesh.shape["scen"], mesh.shape["row"]),
        mesh=mesh, in_specs=placed, out_specs=P("row", None), check_vma=False,
    )
```

```python
import functools

import jax
import jax.numpy as jnp
from jax import lax
from jax.experimental import pallas as pl
from jax.experimental.pallas import tpu as pltpu
from jax.sharding import PartitionSpec as P

PANEL = 128
MESH = pl.DeviceIdType.MESH
HIGH = lax.Precision.HIGHEST
F32 = jnp.float32
BF16 = jnp.bfloat16
PARTS = 3
SUB = 8
BLOCK = 32
MAIN_VMEM = 40 << 20
LAST_VMEM = 8 << 20
STEPS = 32766.0
TINY = 1e-30


def small_factor(spread):
    shape = spread[0].shape
    cell = {
        (i, k): jnp.broadcast_to(spread[k][i:i + 1, :], shape)
        for k in range(SUB) for i in range(k, SUB)
    }
    scale, lower = [], {}
    for j in range(SUB):
        scale.append(lax.rsqrt(cell[j, j]))
        for i in range(j + 1, SUB):
            lower[i, j] = cell[i, j] * scale[j]
        for k in range(j + 1, SUB):
            for i in range(k, SUB):
                cell[i, k] = cell[i, k] - lower[i, j] * lower[k, j]
    inverse = {}
    for j in range(SUB):
        inverse[j, j] = scale[j]
        for i in range(j + 1, SUB):
            total = lower[i, j] * inverse[j, j]
            for m in range(j + 1, i):
                total = total + lower[i, m] * inverse[m, j]
            inverse[i, j] = -(scale[i] * total)
    return inverse, scale, lower


def split2(value):
    high = value.astype(BF16)
    return high, (value - high.astype(F32)).astype(BF16)


def panel_inverse(block, size, hook=None):
    panel = block.shape[0]
    shape = (SUB, panel)
    sub = lax.broadcasted_iota(jnp.int32, shape, 0)
    lane = lax.broadcasted_iota(jnp.int32, shape, 1)
    tiles = panel // SUB
    left = [block[low:low + SUB, :] for low in range(0, panel, SUB)]
    right = [jnp.where(lane == sub + low, 1.0, 0.0) for low in range(0, panel, SUB)]
    per = size // SUB
    for base in range(0, tiles, per):
        spread = {
            (tile, own): [
                jnp.broadcast_to(left[tile][:, at:at + 1], shape)
                for at in range(own * SUB, own * SUB + SUB)
            ]
            for tile in range(base, base + per) for own in range(base, tile + 1)
        }
        for own in range(base, base + per):
            inverse, scale, lower = small_factor(spread[own, own])
            rest = range(own + 1, base + per)
            factors, lines = {}, {}
            for tile in rest:
                column = list(spread[tile, own])
                for k in range(SUB):
                    factor = column[k] * scale[k]
                    for m in range(k + 1, SUB):
                        column[m] = column[m] - factor * lower[m, k]
                    factors[tile, k] = factor
                    for i in range(SUB):
                        lines[tile, k, i] = jnp.broadcast_to(factor[i:i + 1, :], shape)
                for across in range(own + 1, tile + 1):
                    for k in range(SUB):
                        for i in range(SUB):
                            spread[tile, across][i] = (
                                spread[tile, across][i]
                                - factors[tile, k] * lines[across, k, i]
                            )
            new_left = new_right = None
            for k in range(SUB):
                coeff = inverse[SUB - 1, k]
                for i in range(SUB - 2, k - 1, -1):
                    coeff = jnp.where(sub <= i, inverse[i, k], coeff)
                if k:
                    coeff = jnp.where(sub < k, 0.0, coeff)
                add_left = coeff * left[own][k:k + 1, :]
                add_right = coeff * right[own][k:k + 1, :]
                new_left = add_left if k == 0 else new_left + add_left
                new_right = add_right if k == 0 else new_right + add_right
            for tile in rest:
                for k in range(SUB):
                    left[tile] = left[tile] - factors[tile, k] * new_left[k:k + 1, :]
                    right[tile] = right[tile] - factors[tile, k] * new_right[k:k + 1, :]
            left[own], right[own] = new_left, new_right
            if hook is not None:
                hook(own)
        if base + per < tiles:
            upper = jnp.concatenate(left[base:base + per], axis=0)
            both = jnp.concatenate(
                [upper, jnp.concatenate(right[base:base + per], axis=0)], axis=1
            )
            high, low = split2(both)
            change = lax.dot_general(
                jnp.concatenate(
                    [high[:, :panel], high[:, :panel], low[:, :panel]], axis=0
                ),
                jnp.concatenate([high, low, high], axis=0),
                (((0,), (0,)), ((), ())), preferred_element_type=F32,
            )
            for tile in range(base + per, tiles):
                low = tile * SUB
                left[tile] = left[tile] - change[low:low + SUB, :panel]
                right[tile] = right[tile] - change[low:low + SUB, panel:]
    return jnp.concatenate(right, axis=0)


def flip(index, bit):
    return index + bit * (1 - 2 * ((index // bit) % 2))


def toggle(index, mask):
    bit = 1
    while bit <= mask:
        if mask & bit:
            index = flip(index, bit)
        bit *= 2
    return index


def bits_down(count):
    bits = []
    bit = count // 2
    while bit >= 1:
        bits.append(bit)
        bit //= 2
    return bits


def low_bit(mask):
    return mask & -mask


def split3(value):
    high = value.astype(BF16)
    rest = value - high.astype(F32)
    middle = rest.astype(BF16)
    low = (rest - middle.astype(F32)).astype(BF16)
    return high, middle, low


def wide(*mats):
    blocks = []
    for mat in mats:
        high, low = split2(mat)
        blocks.append(jnp.concatenate(
            [jnp.concatenate([high, low], axis=0),
             jnp.concatenate([high, jnp.zeros_like(low)], axis=0)], axis=1))
    return jnp.concatenate(blocks, axis=0)


def product_t(lhs, stacked):
    high, low = split2(lhs)
    both = lax.dot_general(
        jnp.concatenate([high, low], axis=1), stacked, (((1,), (1,)), ((), ())),
        preferred_element_type=F32,
    )
    side = lhs.shape[1]
    return [
        both[:, at:at + side] + both[:, at + side:at + 2 * side]
        for at in range(0, both.shape[1], 2 * side)
    ]


def product(lhs, rhs):
    high, low = split2(lhs)
    top, bottom = split2(rhs)
    both = jnp.dot(
        jnp.concatenate([high, low], axis=1),
        jnp.concatenate(
            [jnp.concatenate([top, bottom], axis=1),
             jnp.concatenate([top, jnp.zeros_like(top)], axis=1)], axis=0),
        preferred_element_type=F32,
    )
    side = rhs.shape[1]
    return both[:, :side] + both[:, side:]


def code(value):
    top = jnp.max(jnp.abs(value), axis=0, keepdims=True)
    unit = jnp.maximum(top, TINY) * (1.0 / STEPS)
    return jnp.round(value * (1.0 / unit)).astype(jnp.int32).astype(jnp.int16), unit


def decode(steps, unit):
    return steps.astype(jnp.int32).astype(F32) * unit


def schur_kernel(
    n_scen, n_row,
    asg, pv_hbm, prob_hbm, bar_hbm, b_hbm, k_hbm, base_hbm,
    left_ref, right_ref, h_ref, stack_ref,
    b_ref, k_ref, base, load_sem, rest_sem, pv_row, pv_s, prob, bar_row, onehot,
    picked, xin, zsum, zin, columns, solved,
    fpick, fxin, fsum, fzin, fall,
    bt, ct, tf, t_sum, t_in, u_own, u_in, u_sum, u_all, mine,
    first_stack, out_half, in_half, steps, units, steps_in, units_in, h_first,
    rsx_send, rsz_send, ca_send, sa_send, rsz_recv, cx_recv, sx_recv,
    rsx_recv, cz_recv, sz_recv,
    t_send, t_recv, u_send, u_recv, c_send, c_recv, y_send, y_recv, g_send, g_recv,
):
    scen = lax.axis_index("scen")
    row = lax.axis_index("row")
    panels = columns.shape[0]
    depth = columns.shape[2]
    full = n_row * depth
    rows, window = base.shape
    nz = n_row // 2
    z, x = row // 2, row % 2
    other = flip(row, 1)
    barrier = pltpu.get_barrier_semaphore()
    scen_bits = bits_down(n_scen)[::-1]
    y_bits = scen_bits[1:]
    near = [toggle(z, step) for step in range(1, nz)]
    far = near[::-1]
    frow = fpick.shape[1]
    frows = n_row * frow
    groups = window // frows
    fstart = (scen % groups) * frows
    first = row * rows
    done = (h_first, h_ref)

    pl.semaphore_signal(barrier, inc=1, device_id={"row": other}, device_id_type=MESH)
    for peer in far:
        pl.semaphore_signal(
            barrier, inc=1, device_id={"row": 2 * peer + x}, device_id_type=MESH
        )
    for bit in scen_bits:
        pl.semaphore_signal(
            barrier, inc=1, device_id={"scen": flip(scen, bit)}, device_id_type=MESH
        )

    def load(block):
        start = pl.multiple_of(block * depth, depth)
        return pltpu.make_async_copy(
            b_hbm.at[pl.ds(start, depth), :],
            b_ref.at[pl.ds(start, depth), :],
            load_sem.at[block],
        )

    base_load = pltpu.make_async_copy(base_hbm, base, rest_sem.at[0])
    k_load = pltpu.make_async_copy(k_hbm, k_ref, rest_sem.at[1])
    small = [
        pltpu.make_async_copy(source, to, rest_sem.at[2 + index])
        for index, (source, to) in enumerate((
            (pv_hbm, pv_row), (bar_hbm, bar_row), (pv_hbm.at[0], pv_s),
            (prob_hbm, prob),
        ))
    ]
    small[0].start()
    for peer in far + [z]:
        load(2 * peer + 1 - x).start()
    for one in small[1:]:
        one.start()
    base_load.start()
    for peer in far + [z]:
        load(2 * peer + x).start()
    k_load.start()

    small[0].wait()
    onehot[...] = jnp.where(
        lax.broadcasted_iota(jnp.int32, (rows, window), 0) == pv_row[...] - first,
        1.0, 0.0,
    ).astype(BF16)
    pl.semaphore_wait(barrier, nz + len(scen_bits))

    def remote(src, dst, send, recv, where):
        return pltpu.make_async_remote_copy(
            src_ref=src, dst_ref=dst, send_sem=send, recv_sem=recv,
            device_id=where, device_id_type=MESH,
        )

    def go(copy):
        copy.start()

    def drained(held, sem):
        remote(held, held, sem, sem, {"row": other}).wait_send()

    pick_of = [picked.at[p] for p in range(panels)] + [fpick]
    xin_of = [xin.at[p] for p in range(panels)] + [fxin]
    zsum_of = [zsum.at[p] for p in range(panels)] + [fsum]
    zin_of = [zin.at[p] for p in range(panels)] + [fzin]
    col_of = [columns.at[p] for p in range(panels)] + [fall]
    sol_of = [solved.at[p] for p in range(panels)]

    def rsx(p, peer):
        return remote(
            pick_of[p].at[2 * peer + 1 - x], xin_of[p].at[peer],
            rsx_send.at[p], rsx_recv.at[p, peer], {"row": other},
        )

    def rsz_go(p, peer):
        go(remote(
            zsum_of[p].at[peer], zin_of[p].at[z],
            rsz_send.at[p], rsz_recv.at[p], {"row": 2 * peer + x},
        ))

    def rsz_wait(p):
        held = zin_of[p].at[pl.ds(0, nz - 1)]
        remote(held, held, rsz_send.at[p], rsz_recv.at[p], {"row": other}).wait_recv()

    def rs_turn(p):
        for peer in far + [z]:
            rsx(p, peer).wait_recv()
            zsum_of[p][peer] = pick_of[p][2 * peer + x] + xin_of[p][peer]
            if peer is not z:
                rsz_go(p, peer)

    def rs_end(p):
        total = zsum_of[p][z].astype(F32)
        rsz_wait(p)
        for peer in near:
            total = total + zin_of[p][peer].astype(F32)
        col_of[p][row] = total.astype(col_of[p].dtype)

    cols = (col_of, ca_send, cz_recv, cx_recv)
    sols = (sol_of, sa_send, sz_recv, sx_recv)

    def ag_x(kind, p, peer):
        held, send, _, xr = kind
        return remote(
            held[p].at[2 * peer + x], held[p].at[2 * peer + x],
            send.at[p], xr.at[p], {"row": other},
        )

    def ag_start(kind, p):
        held, send, zr, _ = kind
        for peer in near:
            go(remote(
                held[p].at[row], held[p].at[row],
                send.at[p], zr.at[p, z], {"row": 2 * peer + x},
            ))
        go(ag_x(kind, p, z))

    def ag_pass(kind, p, peer):
        held, send, zr, _ = kind
        remote(
            held[p].at[2 * peer + x], held[p].at[2 * peer + x],
            send.at[p], zr.at[p, peer], {"row": 2 * peer + x},
        ).wait_recv()
        go(ag_x(kind, p, peer))

    def ag_end(kind, p):
        held, send, _, xr = kind
        some = held[p].at[pl.ds(0, nz)]
        remote(some, some, send.at[p], xr.at[p], {"row": other}).wait_recv()

    def pick(dst):
        load(dst).wait()
        start = pl.multiple_of(dst * depth, depth)
        block = jnp.dot(
            b_ref[pl.ds(start, depth), :], onehot[...], preferred_element_type=F32
        ).astype(BF16)
        for p in range(panels):
            picked[p, dst] = block[:, p * PANEL:(p + 1) * PANEL]

    for peer in far + [z]:
        pick(2 * peer + 1 - x)
        go(rsx(0, peer))
    for p in range(1, panels):
        for peer in far + [z]:
            go(rsx(p, peer))
    for peer in far + [z]:
        pick(2 * peer + x)

    for one in small[1:]:
        one.wait()
    bar = split3(bar_row[...].reshape(1, rows))
    level = lax.broadcasted_iota(jnp.int32, (2 * SUB, rows), 0)
    bars = jnp.where(
        level == 0, bar[0].astype(F32),
        jnp.where(level == 1, bar[1].astype(F32),
                  jnp.where(level == 2, bar[2].astype(F32), 0.0)),
    ).astype(BF16)

    bsel = jnp.sum(
        jnp.dot(bars, onehot[...], preferred_element_type=F32), axis=0, keepdims=True
    )
    base_load.wait()
    slot_row = lax.broadcasted_iota(jnp.int32, (frow, window), 0) + fstart
    slot_col = lax.broadcasted_iota(jnp.int32, (frow, window), 1)

    def frag(block, carry):
        lines = []
        for i in range(frow):
            at = pv_s[fstart + block * frow + i] - first
            inside = jnp.logical_and(at >= 0, at < rows)
            line = base[pl.ds(jnp.clip(at, 0, rows - 1), 1), :]
            lines.append(jnp.where(inside, line, 0.0))
        fpick[block] = jnp.concatenate(lines, axis=0) + jnp.where(
            slot_row + block * frow == slot_col, bsel, 0.0
        )
        return carry

    lax.fori_loop(0, n_row, frag, 0)
    for peer in far + [z]:
        go(rsx(panels, peer))

    for p in range(panels):
        rs_turn(p)

    def turn(tile, carry):
        start = pl.multiple_of(tile * PANEL, PANEL)
        bt[pl.ds(start, PANEL), :] = b_ref[:, pl.ds(start, PANEL)].T
        return carry

    def solve(p):
        solved[p, row] = jnp.dot(
            k_ref[...], columns[p].reshape(full, PANEL), preferred_element_type=F32
        ).astype(BF16)

    def side(p):
        ct[p] = columns[p].reshape(full, PANEL).T

    rs_end(0)
    ag_start(cols, 0)
    tiles = rows // PANEL
    ag_pass(cols, 0, near[0])
    rs_end(1)
    ag_start(cols, 1)
    rs_turn(panels)
    for peer in near[1:]:
        ag_pass(cols, 0, peer)
    base[...] += onehot[...].astype(F32) * bsel
    lax.fori_loop(0, tiles // 4, turn, 0)
    ag_pass(cols, 1, near[0])
    k_load.wait()
    ag_end(cols, 0)
    solve(0)
    ag_start(sols, 0)
    rs_end(panels)
    ag_start(cols, panels)
    for peer in near[1:]:
        ag_pass(cols, 1, peer)
    lax.fori_loop(tiles // 4, tiles, turn, 0)
    side(0)
    ag_pass(sols, 0, near[0])
    ag_end(cols, 1)
    solve(1)
    ag_start(sols, 1)
    for peer in near:
        ag_pass(cols, panels, peer)
    for peer in near[1:]:
        ag_pass(sols, 0, peer)
    side(1)
    for peer in near[:-1]:
        ag_pass(sols, 1, peer)
    ag_end(cols, panels)
    tf[...] = jnp.zeros_like(tf)
    keep = jnp.where(scen < groups, 1.0, 0.0)
    tf[pl.ds(pl.multiple_of(fstart, SUB), frows), :] = fall[...].reshape(frows, window) * keep
    weight = prob[asg[0]]

    def t_block(p, q):
        return weight * jnp.dot(
            ct[p], solved[q].reshape(full, PANEL), preferred_element_type=F32
        ) + tf[p * PANEL:(p + 1) * PANEL, q * PANEL:(q + 1) * PANEL]

    core = scen % 2
    pair = {"scen": flip(scen, 1)}
    bits = range(len(scen_bits))

    def shared(own, into, sums, total, send, recv):
        size = own.shape[0] // 2
        here = pl.ds(pl.multiple_of(core * size, SUB), size)
        there = pl.ds(pl.multiple_of((1 - core) * size, SUB), size)
        final = len(scen_bits)

        def copy(index):
            return remote(
                own.at[there, :] if index == 0 else sums.at[index - 1],
                total.at[here, :] if index == final else into.at[index],
                send.at[index], recv.at[index],
                {"scen": flip(scen, scen_bits[index % final])},
            )

        def step(index):
            copy(index).wait_recv()
            before = own[here, :] if index == 0 else sums[index - 1]
            sums[index] = before + into[index]
            go(copy(index + 1))
            if index + 1 == final:
                total[here, :] = sums[index]

        def end():
            remote(
                sums.at[0], total.at[there, :], send.at[final], recv.at[final], pair
            ).wait_recv()

        return copy, step, end

    def t_copy(index):
        return remote(
            t_sum.at[index], t_in.at[index], t_send.at[index], t_recv.at[index],
            {"scen": flip(scen, scen_bits[index])},
        )

    def t_step(index):
        t_copy(index).wait_recv()
        t_sum[index + 1] = t_sum[index] + t_in[index]
        if index + 1 < len(scen_bits):
            go(t_copy(index + 1))

    u_copy, u_step, u_end = shared(u_own, u_in, u_sum, u_all, u_send, u_recv)

    half = rows // 2
    chunk = half // PARTS
    parts = range(PARTS)

    def place(which, part):
        return pl.ds(pl.multiple_of(which * half + part * chunk, SUB), chunk)

    def term(which, p, part):
        return weight * jnp.dot(
            bt[place(which, part), :], solved[p].reshape(full, PANEL),
            preferred_element_type=F32,
        )

    def c_copy(p, part):
        return remote(
            out_half.at[p, part], in_half.at[p, part],
            c_send.at[0], c_recv.at[p, part], {"scen": flip(scen, 1)},
        )

    def y_copies(index, p, part):
        where = {"scen": flip(scen, y_bits[index])}
        return (
            remote(
                steps.at[index, p, part], steps_in.at[index, p, part],
                y_send.at[0], y_recv.at[0, index, p, part], where,
            ),
            remote(
                units.at[index, p, part], units_in.at[index, p, part],
                y_send.at[1], y_recv.at[1, index, p, part], where,
            ),
        )

    def y_code(index, p, part, value):
        steps[index, p, part], unit = code(value)
        units[index, p, part] = jnp.broadcast_to(unit, units.shape[3:])

    def y_go(index, p, part):
        for one in y_copies(index, p, part):
            go(one)

    def g_copy(p, part, which):
        return remote(
            done[p].at[place(which, part), :], done[p].at[place(which, part), :],
            g_send.at[p], g_recv.at[p], {"scen": flip(scen, 1)},
        )

    def h_out(p):
        for part in parts:
            out_half[p, part] = term(1 - core, p, part)

    def h_own(p):
        for part in parts:
            mine[part] = term(core, p, part)

    def c_go(p):
        for part in parts:
            go(c_copy(p, part))

    def h_join(p, part):
        y_code(0, p, part, mine[part] + in_half[p, part])

    def y_wait(p, part):
        for index in range(len(y_bits)):
            for one in y_copies(index, p, part):
                one.wait_recv()
            if index + 1 < len(y_bits):
                y_code(index + 1, p, part, y_total(index, p, part))
                y_go(index + 1, p, part)

    def y_total(index, p, part):
        return decode(
            steps[index, p, part], units[index, p, part][0:1, :]
        ) + decode(steps_in[index, p, part], units_in[index, p, part][0:1, :])

    def h_end(p, part):
        done[p][place(core, part), :] = (
            y_total(len(y_bits) - 1, p, part)
            + base[place(core, part), p * PANEL:(p + 1) * PANEL]
        )

    ag_end(sols, 0)
    whole = t_block(0, 0)
    t_sum[0] = 0.5 * (whole + whole.T)
    go(t_copy(0))
    for peer in near[-1:]:
        ag_pass(sols, 1, peer)
    t_step(0)
    h_out(0)
    c_go(0)
    h_own(0)
    for part in parts[:2]:
        c_copy(0, part).wait_recv()
        h_join(0, part)
        y_go(0, 0, part)
    for part in parts[2:]:
        c_copy(0, part).wait_recv()
        h_join(0, part)
    ag_end(sols, 1)
    u_own[:PANEL, :] = 0.5 * (t_block(1, 0) + t_block(0, 1).T)
    whole = t_block(1, 1)
    u_own[PANEL:, :] = 0.5 * (whole + whole.T)
    go(u_copy(0))
    for index in bits[1:]:
        t_step(index)

    def hook_0(tile):
        if tile == 1:
            u_step(0)
            for part in parts[2:]:
                y_go(0, 0, part)
            h_out(1)
        elif tile == 4:
            c_go(1)
            h_own(1)
        elif tile == 8:
            for part in parts:
                c_copy(1, part).wait_recv()
            for part in parts:
                h_join(1, part)
        elif tile == 11:
            for part in parts:
                y_go(0, 1, part)
        elif tile == 14:
            for index in bits[1:]:
                u_step(index)

    inverse_0 = panel_inverse(t_sum[len(scen_bits)], BLOCK, hook_0)
    for part in parts[:2]:
        y_wait(0, part)
        h_end(0, part)
        go(g_copy(0, part, core))
    u_end()
    lower = product_t(u_all[:PANEL, :], wide(inverse_0))[0]
    block = u_all[PANEL:, :] - product_t(lower, wide(lower))[0]

    def g_end(p):
        some = done[p].at[pl.ds(0, half), :]
        remote(some, some, g_send.at[p], g_recv.at[p], pair).wait_recv()

    def drop(which, part):
        left, right = product_t(h_first[place(which, part), :], first_stack[...])
        left_ref[place(which, part), :] = left
        right_ref[place(which, part), :] = right

    def hook(tile):
        if tile == 0:
            first_stack[...] = wide(inverse_0, product(lower, inverse_0))
        elif tile == 2:
            for part in parts[2:]:
                y_wait(0, part)
            for part in parts[2:]:
                h_end(0, part)
        elif tile == 4:
            for part in parts[2:]:
                go(g_copy(0, part, core))
            for part in parts:
                drop(core, part)
        elif tile == 8:
            g_end(0)
            for part in parts:
                drop(1 - core, part)
        elif tile == 11:
            for part in parts[:2]:
                y_wait(1, part)
            for part in parts[:2]:
                h_end(1, part)
        elif tile == 13:
            for part in parts[:2]:
                go(g_copy(1, part, core))
            for part in parts[2:]:
                y_wait(1, part)
            for part in parts[2:]:
                h_end(1, part)
        elif tile == 14:
            for part in parts[2:]:
                go(g_copy(1, part, core))

    stack_ref[...] = wide(panel_inverse(block, BLOCK, hook))
    g_end(1)
    for p in range(panels + 1):
        drained(xin_of[p], rsx_send.at[p])
        drained(zin_of[p].at[pl.ds(0, nz - 1)], rsz_send.at[p])
        drained(col_of[p].at[pl.ds(0, n_row - 1)], ca_send.at[p])
    for p in range(panels):
        drained(sol_of[p].at[pl.ds(0, n_row - 1)], sa_send.at[p])
        drained(done[p].at[pl.ds(0, half), :], g_send.at[p])
    for index in bits:
        t_copy(index).wait_send()
    for index in range(len(scen_bits) + 1):
        u_copy(index).wait_send()
    drained(out_half, c_send.at[0])
    drained(steps, y_send.at[0])
    drained(units, y_send.at[1])


def last_kernel(pieces, left_ref, right_ref, h_ref, stack_ref, out_hbm, out, sem):
    size = out.shape[0] // pieces

    def store(side, piece, source):
        return pltpu.make_async_copy(
            source.at[pl.ds(piece * size, size), :],
            out_hbm.at[pl.ds(piece * size, size), pl.ds(side * PANEL, PANEL)],
            sem.at[side, piece],
        )

    for piece in range(pieces):
        store(0, piece, left_ref).start()
    for piece in range(pieces):
        span = pl.ds(piece * size, size)
        out[span, :] = product_t(h_ref[span, :] - right_ref[span, :], stack_ref[...])[0]
        store(1, piece, out).start()
    for piece in range(pieces):
        store(0, piece, left_ref).wait()
        store(1, piece, out).wait()


def per_device(
    n_scen, n_row,
    borders, kkt_inverse, first_section, barrier, panel_vars, probability, assignment,
):
    rows, window = first_section.shape
    depth = kkt_inverse.shape[1]
    full = kkt_inverse.shape[2]
    panels = window // PANEL
    nz = n_row // 2
    groups = max(1, min(n_scen, window // (8 * n_row)))
    frow = window // groups // n_row
    stages = n_scen.bit_length() - 1
    chunk = rows // 2 // PARTS
    dma = pltpu.SemaphoreType.DMA
    vmem = pl.BlockSpec(memory_space=pltpu.VMEM)

    def buf(shape, dtype):
        return pltpu.VMEM(shape, dtype)

    held = pl.pallas_call(
        functools.partial(schur_kernel, n_scen, n_row),
        out_shape=(
            buf((rows, PANEL), F32), buf((rows, PANEL), F32), buf((rows, PANEL), F32),
            buf((2 * PANEL, 2 * PANEL), BF16),
        ),
        in_specs=[pl.BlockSpec(memory_space=pltpu.SMEM)]
        + [pl.BlockSpec(memory_space=pltpu.HBM)] * 6,
        out_specs=(vmem,) * 4,
        scratch_shapes=[
            buf((full, rows), BF16), buf((depth, full), BF16), buf((rows, window), F32),
            dma((n_row,)), dma((6,)),
            buf((1, window), jnp.int32), pltpu.SMEM((window,), jnp.int32),
            pltpu.SMEM((n_scen,), F32), buf((rows,), F32),
            buf((rows, window), BF16),
            buf((panels, n_row, depth, PANEL), BF16),
            buf((panels, nz, depth, PANEL), BF16),
            buf((panels, nz, depth, PANEL), BF16),
            buf((panels, nz, depth, PANEL), BF16),
            buf((panels, n_row, depth, PANEL), BF16),
            buf((panels, n_row, depth, PANEL), BF16),
            buf((n_row, frow, window), F32),
            buf((nz, frow, window), F32),
            buf((nz, frow, window), F32),
            buf((nz, frow, window), F32),
            buf((n_row, frow, window), F32),
            buf((rows, full), BF16), buf((panels, PANEL, full), BF16),
            buf((window, window), F32),
            buf((stages + 1, PANEL, PANEL), F32), buf((stages, PANEL, PANEL), F32),
            buf((2 * PANEL, PANEL), F32), buf((stages, PANEL, PANEL), F32),
            buf((stages, PANEL, PANEL), F32), buf((2 * PANEL, PANEL), F32),
            buf((PARTS, chunk, PANEL), F32),
            buf((4 * PANEL, 2 * PANEL), BF16),
            buf((panels, PARTS, chunk, PANEL), F32),
            buf((panels, PARTS, chunk, PANEL), F32),
            *[buf((stages - 1, panels, PARTS, chunk, PANEL), jnp.int16),
              buf((stages - 1, panels, PARTS, SUB, PANEL), F32)] * 2,
            buf((rows, PANEL), F32),
            *[dma((panels + 1,))] * 3, dma((panels,)), *[dma((panels + 1,))] * 2,
            dma((panels,)), *[dma((panels + 1, nz))] * 2, dma((panels, nz)),
            *[dma((stages,))] * 2, *[dma((stages + 1,))] * 2,
            dma((1,)), dma((panels, PARTS)),
            dma((2,)), dma((2, stages - 1, panels, PARTS)),
            *[dma((panels,))] * 2,
        ],
        compiler_params=pltpu.CompilerParams(
            collective_id=0, has_side_effects=True, vmem_limit_bytes=MAIN_VMEM
        ),
    )(
        assignment,
        *[pltpu.with_memory_space_constraint(one, pltpu.HBM)
          for one in (panel_vars[None, :], probability, barrier,
                      borders[0], kkt_inverse[0], first_section)],
    )
    pieces = 2 * PARTS
    return pl.pallas_call(
        functools.partial(last_kernel, pieces),
        out_shape=jax.ShapeDtypeStruct((rows, window), F32),
        in_specs=[vmem] * 4,
        out_specs=pl.BlockSpec(memory_space=pl.ANY),
        scratch_shapes=[buf((rows, PANEL), F32), dma((2, pieces))],
        compiler_params=pltpu.CompilerParams(vmem_limit_bytes=LAST_VMEM),
    )(*[pltpu.with_memory_space_constraint(one, pltpu.VMEM) for one in held])


def solution(mesh):
    placed = (
        P("scen", None, "row"),
        P("scen", "row", None),
        P("row", None),
        P("row"),
        P(),
        P(),
        P("scen"),
    )
    return jax.shard_map(
        functools.partial(per_device, mesh.shape["scen"], mesh.shape["row"]),
        mesh=mesh, in_specs=placed, out_specs=P("row", None), check_vma=False,
    )
```
